256 devices in a mesh: dp: 8 (over z), tensor: 32 (over x, y, core).
Axes of the slice: x: 4, y: 4, z: 8, core: 2. Of those that a mesh axis runs over, the one named last changes fastest.
Arguments:
- activations: bfloat16 [2048, 27648], P('dp', 'tensor'), may hold values from -6 to 6
- left_factor: float32 [216, 216], replicated, may hold values from -2 to 3, as said below
- right_factor: float32 [128, 128], replicated, may hold values from -2 to 3, as said below
- clip_scale: float32 [128, 216], replicated, may hold values from 0.5 to 3
- weight_rows: bfloat16 [27648, 5120], P('tensor'), may hold values from -0.0390625 to 0.0390625
- target: bfloat16 [2048, 5120], P('dp'), may hold values from -6 to 6
Outputs:
- grad_left: float32 [216, 216], replicated
- grad_right: float32 [128, 128], replicated
- grad_input: float32 [2048, 27648], P('dp', 'tensor')
The draws below stay inside these ranges and needn't reach their ends.
Inputs may be any that keep to these rules, and one draw needn't show every extreme that they name: `left_factor`: the identity plus independent entries of order one over the square root of 216. `right_factor`: the identity plus independent entries of order one over the square root of 128.
All inputs are finite; a program needn't handle non-finite values.
Results may differ from the reference program's by a relative error of at most 0.007.
Values may be sent and summed in bfloat16 or wider, within the bound.
No kernel may reach another device: no remote copies, remote signals or barrier semaphores. Data moves between devices by JAX's collectives and lax.ppermute only.
A program may use at most 64 MiB of HBM per device.

```python
import math
import jax
import jax.numpy as jnp
from jax import lax

OUT = 5120
F1 = 216
F2 = 128
HID = 27648
TOKENS = 2048


def make_factor(key, order):
    noise = jnp.clip(jax.random.normal(key, (order, order), jnp.float32), -4.0, 4.0)
    return jnp.eye(order, dtype=jnp.float32) + noise / jnp.sqrt(order * 1.0)


def draw_left_factor(key, part):
    return make_factor(jax.random.fold_in(key, 11), F1)


def draw_right_factor(key, part):
    return make_factor(jax.random.fold_in(key, 23), F2)


def block_levels(key, shape, pieces, low, high):
    def one(dim, blocks):
        steps = jax.random.uniform(jax.random.fold_in(jax.random.fold_in(key, 6), dim), (blocks,), jnp.float32, low / len(pieces), high / len(pieces))
        return jnp.repeat(jnp.exp(steps), shape[dim] // blocks).reshape((-1,) + (1,) * (len(shape) - dim - 1))

    factor_of = one(*pieces[0])
    for cut in pieces[1:]:
        factor_of = factor_of * one(*cut)
    return factor_of


def normal_values(stream_key, shape, spread, bound, pieces=(), kind=jnp.bfloat16):
    loudness = block_levels(stream_key, shape, pieces, -0.22, 0.18) if pieces else 1.0
    values = jax.random.normal(stream_key, shape, jnp.float32) * spread * loudness
    return jnp.minimum(jnp.maximum(values, -bound), bound).astype(kind)


def setup_inputs(seed: int = 0) -> dict:
    seeds = jax.random.split(jax.random.key(seed), 7)
    activations = normal_values(seeds[0], (TOKENS, HID), 1.0, 6.0, ((0, 8), (1, 32)))
    left_factor = draw_left_factor(jax.random.fold_in(seeds[6], 71), 0)
    right_factor = draw_right_factor(jax.random.fold_in(seeds[6], 71), 0)
    clip_scale = jnp.clip(jnp.exp(jax.random.uniform(seeds[3], (F2, F1), jnp.float32, math.log(0.5), math.log(3.0))), 0.5, 3.0)
    weight_rows = normal_values(seeds[4], (HID, OUT), HID ** -0.5, 0.0390625, ((0, 32),))
    target = normal_values(seeds[5], (TOKENS, OUT), 1.0, 6.0, ((0, 8),))
    return dict(activations=activations, left_factor=left_factor, right_factor=right_factor, clip_scale=clip_scale, weight_rows=weight_rows, target=target)


def reference(activations, left_factor, right_factor, clip_scale, weight_rows, target):
    highest = lax.Precision.HIGHEST
    inputs = activations.reshape(TOKENS, F2, F1).astype(jnp.float32)
    mixed = jnp.einsum('tji,ik->tjk', inputs, left_factor, precision=highest)
    rotated = jnp.einsum('jl,tjk->tlk', right_factor, mixed, precision=highest)
    bounded = jnp.tanh(rotated / clip_scale)
    clipped = (clip_scale * bounded).astype(jnp.bfloat16).reshape(TOKENS, HID)
    output = jnp.dot(clipped, weight_rows, preferred_element_type=jnp.float32)
    out_grad = (output - target.astype(jnp.float32)).astype(jnp.bfloat16)
    clipped_grad = lax.dot_general(out_grad, weight_rows, (((1,), (1,)), ((), ())), preferred_element_type=jnp.float32)
    rotated_grad = clipped_grad.reshape(TOKENS, F2, F1) * (1.0 - bounded * bounded)
    mixed_grad = jnp.einsum('jl,tlk->tjk', right_factor, rotated_grad, precision=highest)
    grad_right = jnp.einsum('tjk,tlk->jl', mixed, rotated_grad, precision=highest)
    grad_left = jnp.einsum('tji,tjk->ik', inputs, mixed_grad, precision=highest)
    grad_input = jnp.einsum('tjk,ik->tji', mixed_grad, left_factor, precision=highest).reshape(TOKENS, HID)
    return grad_left, grad_right, grad_input
```

```python
import functools

import jax
import jax.numpy as jnp
from jax import lax
from jax.experimental import pallas as pl
from jax.experimental.pallas import tpu as pltpu
from jax.sharding import Mesh
from jax.sharding import PartitionSpec as P

CHIPS = ("chip_x", "chip_y")
TENSOR = (*CHIPS, "core")
F32, BF16 = jnp.float32, jnp.bfloat16
TN = (((0,), (0,)), ((), ()))
NT = (((1,), (1,)), ((), ()))
NN = (((1,), (0,)), ((), ()))

LANES, WIDE = 128, 256
TOK = 8


def call(kernel, outs, name, flops=0, moved=0, vmem=48, **kw):
    return pl.pallas_call(
        kernel,
        out_shape=outs,
        compiler_params=pltpu.CompilerParams(vmem_limit_bytes=vmem << 20),
        cost_estimate=pl.CostEstimate(flops=flops, bytes_accessed=moved, transcendentals=0),
        name=name,
        **kw,
    )


def shape(*lengths, dtype=BF16):
    return jax.ShapeDtypeStruct(lengths, dtype)


def halves(a):
    high = a.astype(BF16)
    return high, (a - high.astype(F32)).astype(BF16)


def dot(a, b, dims):
    return lax.dot_general(a, b, dims, preferred_element_type=F32)


def dot3(a, b, dims):
    (a_high, a_low), (b_high, b_low) = a, b
    return dot(a_high, b_high, dims) + (dot(a_high, b_low, dims) + dot(a_low, b_high, dims))


def of_token(ref, token, count):
    rows = pl.ds(token, count, stride=TOK)
    return jnp.concatenate([ref[0, rows, :], ref[1, rows, :]], axis=1)


def put_token(ref, token, value):
    rows = pl.ds(token, value.shape[0], stride=TOK)
    ref[0, rows, :] = value[:, :LANES]
    ref[1, rows, :] = value[:, LANES:]


def joined(ref):
    return jnp.concatenate([ref[0], ref[1]], axis=1)


def widened(a, rows, value=0.0):
    return jnp.pad(a, ((0, rows - a.shape[0]), (0, WIDE - a.shape[1])), constant_values=value)


def by_token_kernel(width, x_ref, o_ref):
    for j in range(o_ref.shape[2]):
        part = x_ref[j * width : (j + 1) * width, :].astype(F32)
        part = jnp.pad(part, ((0, WIDE - width), (0, 0)))
        turned = part.T.astype(BF16)
        half = turned.shape[0] // 2
        for core in range(2):
            o_ref[:, core, j] = turned[core * half : (core + 1) * half].reshape(-1, TOK, WIDE)


def forward_kernel(x_ref, left_ref, right_ref, scale_ref, clip_ref, slope_ref, mixed_ref, hold_ref):
    right_count = right_ref.shape[0]
    left_high, left_low = halves(widened(left_ref[...], WIDE))
    x = x_ref[...]
    mixed = dot(x, left_high, NN) + dot(x, left_low, NN)
    mixed_ref[0] = mixed[:, :LANES]
    mixed_ref[1] = mixed[:, LANES:]
    turned = halves(right_ref[...].T)
    scale = widened(scale_ref[...].T, right_count, 1.0)
    inverse = 1.0 / scale
    for t in range(TOK):
        rotated = dot3(turned, halves(of_token(mixed_ref, t, right_count)), NN)
        bounded = jnp.tanh(rotated * inverse)
        put_token(hold_ref, t, scale * bounded)
        put_token(slope_ref, t, 1.0 - bounded * bounded)
    clip_ref[...] = joined(hold_ref).astype(BF16)


def project_kernel(width, core_ref, clip_ref, own_ref, other_ref, o_ref):
    core = core_ref[0]
    chips = clip_ref.shape[0]
    each = own_ref.shape[0] // width
    total = None
    for ref, base in ((own_ref, core * each), (other_ref, (1 - core) * each)):
        for j in range(each):
            start = pl.multiple_of((base + j) * TOK, TOK)
            part = clip_ref[:, pl.ds(start, TOK), :].reshape(chips * TOK, WIDE)
            term = dot(part[:, :width], ref[j * width : (j + 1) * width, :], NN)
            total = term if total is None else total + term
    o_ref[...] = total.astype(BF16)


def residual_kernel(parts_ref, target_ref, o_ref):
    total = jnp.sum(parts_ref[...].astype(F32), axis=0)
    grad = (total - target_ref[...].astype(F32)).astype(BF16)
    o_ref[...] = jnp.broadcast_to(grad[None], o_ref.shape)


def back_project_kernel(core_ref, grad_ref, own_ref, other_ref, o_ref):
    step = pl.program_id(0)
    each = pl.num_programs(0) // 2
    core = core_ref[0]
    chips = o_ref.shape[0]

    def put(ref, index):
        part = dot(grad_ref[...], ref[...], NT)
        part = widened(part, part.shape[0]).astype(BF16)
        start = pl.multiple_of(index * TOK, TOK)
        o_ref[:, pl.ds(start, TOK), :] = part.reshape(chips, TOK, WIDE)

    @pl.when(step < each)
    def _():
        put(own_ref, core * each + step)

    @pl.when(step >= each)
    def _():
        put(other_ref, (1 - core) * each + step - each)


def backward_kernel(width, grad_ref, slope_ref, mixed_ref, x_ref, right_ref, o_ref, hold_ref, back_ref):
    right_count = right_ref.shape[0]
    owners = o_ref.shape[0]
    own_rows = x_ref.shape[0] // owners
    for side in range(2):
        lanes = slice(side * LANES, (side + 1) * LANES)
        hold_ref[side] = grad_ref[:, lanes].astype(F32) * slope_ref[side]
    right = halves(right_ref[...])
    grad_right = None
    for t in range(TOK):
        rotated_grad = halves(of_token(hold_ref, t, right_count))
        put_token(back_ref, t, dot3(right, rotated_grad, NN))
        term = dot3(halves(of_token(mixed_ref, t, right_count)), rotated_grad, NT)
        grad_right = term if grad_right is None else grad_right + term
    high, low = halves(joined(back_ref))
    x = x_ref[...]
    grad_left = dot(x, high, TN) + dot(x, low, TN)
    o_ref[:, :own_rows, :] = high.reshape(owners, own_rows, WIDE)
    o_ref[:, own_rows:, :] = jnp.zeros((owners, 2 * TOK, WIDE), BF16)
    left_count, right_rows = width // TOK, right_count // TOK
    o_ref[:left_count, own_rows : own_rows + TOK, :] = (
        grad_left[:width].reshape(left_count, TOK, WIDE).astype(BF16)
    )
    o_ref[:right_rows, own_rows + TOK :, :right_count] = grad_right.reshape(
        right_rows, TOK, right_count
    ).astype(BF16)


def input_grad_kernel(back_ref, left_ref, o_ref, factor_ref):
    chips, _, total, _ = back_ref.shape
    width = left_ref.shape[0]
    count = total // TOK - 2
    left_high, left_low = halves(widened(left_ref[...], width))
    half = chips * TOK
    for j in range(count):
        for core in range(2):
            part = back_ref[:, core, j * TOK : (j + 1) * TOK, :].reshape(half, WIDE)
            o_ref[j * width : (j + 1) * width, core * half : (core + 1) * half] = dot(
                left_high, part, NT
            ) + dot(left_low, part, NT)
    factors = back_ref[:, :, count * TOK :, :].astype(F32)
    factor_ref[...] = jnp.broadcast_to(jnp.sum(factors, axis=(0, 1))[None], factor_ref.shape)


def sum_and_copy_kernel(parts_ref, o_ref):
    o_ref[...] = jnp.broadcast_to(jnp.sum(parts_ref[...], axis=0)[None], o_ref.shape)


def unpack_kernel(parts_ref, left_ref, right_ref):
    width, count = left_ref.shape[0], right_ref.shape[0]
    left_ref[...] = parts_ref[: width // TOK, :TOK, :].reshape(width, WIDE)[:, :width]
    right_ref[...] = parts_ref[: count // TOK, TOK:, :count].reshape(count, count)


def exchange(array, axes):
    return lax.all_to_all(array, axes, split_axis=0, concat_axis=0, tiled=True)


def local(activations, left_factor, right_factor, clip_scale, weight_rows, target):
    tokens, hidden = activations.shape
    width, right_count = left_factor.shape[0], right_factor.shape[0]
    columns = weight_rows.shape[1]
    each = hidden // width
    chips = lax.axis_size(CHIPS)
    owners = 2 * chips
    half = tokens // 2
    rows = right_count * TOK
    core = lax.axis_index("core")
    core_operand = core.reshape(1)

    other_rows = lax.ppermute(weight_rows, "core", [(0, 1), (1, 0)])

    by_token = call(
        functools.partial(by_token_kernel, width),
        shape(chips, 2, each, TOK, WIDE), "by_token", 0, 4 * tokens * hidden
    )(activations.T)
    moved = exchange(by_token.reshape(owners, each * TOK, WIDE), TENSOR).reshape(rows, WIDE)

    lanes_apart = shape(2, rows, LANES, dtype=F32)
    hold = pltpu.VMEM((2, rows, LANES), F32)
    clipped, slope, mixed = call(
        forward_kernel,
        (shape(rows, WIDE), lanes_apart, lanes_apart),
        "forward",
        4 * rows * width * width + 6 * rows * width * right_count,
        12 * rows * width,
        scratch_shapes=[hold],
    )(moved, left_factor, right_factor, clip_scale.T)
    clipped_back = exchange(clipped.reshape(chips, 2 * each * TOK, WIDE), CHIPS)

    block = 1024
    smem = pl.BlockSpec(memory_space=pltpu.SMEM)
    partial_out = call(
        functools.partial(project_kernel, width),
        shape(half, columns),
        "project",
        4 * half * hidden * columns,
        4 * hidden * columns,
        grid=(columns // block,),
        in_specs=[
            smem,
            pl.BlockSpec((chips, 2 * each * TOK, WIDE), lambda i: (0, 0, 0)),
            pl.BlockSpec((hidden, block), lambda i: (0, i)),
            pl.BlockSpec((hidden, block), lambda i: (0, i)),
        ],
        out_specs=pl.BlockSpec((half, block), lambda i: (0, i)),
    )(core_operand, clipped_back, weight_rows, other_rows)
    arrived = exchange(partial_out.reshape(chips, TOK, columns), CHIPS)

    own = core * half + lax.axis_index(CHIPS) * TOK
    own_target = lax.dynamic_slice_in_dim(target, own, TOK, 0)
    grad_copies = call(
        residual_kernel, shape(chips, TOK, columns), "residual", 0, 4 * half * columns
    )(arrived, own_target)
    out_grad = exchange(grad_copies, CHIPS).reshape(half, columns)

    clipped_grad = call(
        back_project_kernel,
        shape(chips, 2 * each * TOK, WIDE),
        "back_project",
        4 * half * hidden * columns,
        4 * hidden * columns,
        grid=(2 * each,),
        in_specs=[
            smem,
            pl.BlockSpec((half, columns), lambda i: (0, 0)),
            pl.BlockSpec((width, columns), lambda i: (jnp.minimum(i, each - 1), 0)),
            pl.BlockSpec((width, columns), lambda i: (jnp.maximum(i - each, 0), 0)),
        ],
        out_specs=pl.BlockSpec((chips, 2 * each * TOK, WIDE), lambda i: (0, 0, 0)),
    )(core_operand, out_grad, weight_rows, other_rows)
    grad_owned = exchange(clipped_grad, CHIPS).reshape(rows, WIDE)

    per_owner = (each + 2) * TOK
    packed = call(
        functools.partial(backward_kernel, width),
        shape(owners, per_owner, WIDE),
        "backward",
        4 * rows * width * width + 12 * rows * width * right_count,
        14 * rows * width,
        scratch_shapes=[hold, hold],
    )(grad_owned, slope, mixed, moved, right_factor)
    back = exchange(packed, TENSOR).reshape(chips, 2, per_owner, WIDE)

    groups = lax.axis_size("dp")
    input_grad, factor_copies = call(
        input_grad_kernel,
        (shape(hidden, tokens, dtype=F32), shape(groups, 2 * TOK, WIDE, dtype=F32)),
        "input_grad",
        4 * tokens * hidden * width,
        6 * tokens * hidden,
    )(back, left_factor)
    factor_parts = exchange(factor_copies, "dp")
    factor_sums = call(
        sum_and_copy_kernel, shape(owners, 2 * TOK, WIDE, dtype=F32), "sum_and_copy", 0, 1 << 20
    )(factor_parts)
    gathered = exchange(factor_sums, TENSOR)
    left_sum, right_sum = call(
        unpack_kernel,
        (shape(width, width, dtype=F32), shape(right_count, right_count, dtype=F32)),
        "unpack",
        0,
        1 << 19,
    )(gathered)
    return left_sum, right_sum, input_grad.T


def solution(mesh):
    torus = Mesh(mesh.devices.reshape(mesh.shape["dp"], 4, 4, 2), ("dp", *TENSOR))
    placed = (P("dp", TENSOR), P(), P(), P(), P(TENSOR, None), P("dp", None))
    return jax.shard_map(
        local, mesh=torus, in_specs=placed, out_specs=(P(), P(), P("dp", TENSOR)), check_vma=False
    )
```

```python
import functools

import jax
import jax.numpy as jnp
from jax import lax
from jax.experimental import pallas as pl
from jax.experimental.pallas import tpu as pltpu
from jax.sharding import Mesh
from jax.sharding import PartitionSpec as P

CHIPS = ("chip_x", "chip_y")
TENSOR = (*CHIPS, "core")
F32, BF16 = jnp.float32, jnp.bfloat16
HBM = pltpu.MemorySpace.HBM
TN = (((0,), (0,)), ((), ()))
NT = (((1,), (1,)), ((), ()))
NN = (((1,), (0,)), ((), ()))

LANES, WIDE = 128, 256
TOK = 8


def call(kernel, outs, name, flops=0, moved=0, vmem=16, **kw):
    return pl.pallas_call(
        kernel,
        out_shape=outs,
        compiler_params=pltpu.CompilerParams(vmem_limit_bytes=vmem << 20),
        cost_estimate=pl.CostEstimate(flops=flops, bytes_accessed=moved, transcendentals=0),
        name=name,
        **kw,
    )


def shape(*lengths, dtype=BF16):
    return jax.ShapeDtypeStruct(lengths, dtype)


def halves(a):
    high = a.astype(BF16)
    return high, (a - high.astype(F32)).astype(BF16)


def dot(a, b, dims):
    return lax.dot_general(a, b, dims, preferred_element_type=F32)


def dot3(a, b, dims):
    (a_high, a_low), (b_high, b_low) = a, b
    return dot(a_high, b_high, dims) + (dot(a_high, b_low, dims) + dot(a_low, b_high, dims))


def of_token(ref, token, count):
    rows = pl.ds(token, count, stride=TOK)
    return jnp.concatenate([ref[0, rows, :], ref[1, rows, :]], axis=1)


def put_token(ref, token, value):
    rows = pl.ds(token, value.shape[0], stride=TOK)
    ref[0, rows, :] = value[:, :LANES]
    ref[1, rows, :] = value[:, LANES:]


def joined(ref):
    return jnp.concatenate([ref[0], ref[1]], axis=1)


def widened(a, rows, value=0.0):
    return jnp.pad(a, ((0, rows - a.shape[0]), (0, WIDE - a.shape[1])), constant_values=value)


def first_kernel(width, *refs):
    *sources, o_ref, left_ref, right_ref, scale_ref = refs[:8]
    *buffers, sems = refs[8:]
    x_hbm, x_buf = sources[0], buffers[0]
    count = x_hbm.shape[0] // width
    tall = 2 * width
    cuts = [pl.ds(i * tall, tall) for i in range(count // 2)]
    pairs = [(x_hbm.at[cut], x_buf.at[cut]) for cut in cuts] + list(zip(sources[1:], buffers[1:]))
    copies = [
        pltpu.make_async_copy(src, dst, sems.at[i]) for i, (src, dst) in enumerate(pairs)
    ]
    for copy in copies:
        copy.start()
    for j in range(count):
        if j % 2 == 0:
            copies[j // 2].wait()
        part = x_buf[j * width : (j + 1) * width, :].astype(F32)
        part = jnp.pad(part, ((0, WIDE - width), (0, 0)))
        turned = part.T.astype(BF16)
        half = turned.shape[0] // 2
        for core in range(2):
            o_ref[:, core, j] = turned[core * half : (core + 1) * half].reshape(-1, TOK, WIDE)
    for copy in copies[count // 2 :]:
        copy.wait()
    _, left_buf, right_buf, scale_buf = buffers
    left_ref[0], left_ref[1] = halves(widened(left_buf[...], WIDE))
    right_ref[0], right_ref[1] = halves(right_buf[...])
    right_ref[2], right_ref[3] = halves(right_buf[...].T)
    scale = widened(scale_buf[...].T, right_buf.shape[0], 1.0)
    scale_ref[0] = scale
    scale_ref[1] = 1.0 / scale


def forward_kernel(x_ref, left_ref, right_ref, scale_ref, clip_ref, slope_ref, mixed_ref, hold_ref):
    right_count = right_ref.shape[1]
    x = x_ref[...]
    mixed = dot(x, left_ref[0], NN) + dot(x, left_ref[1], NN)
    mixed_ref[0] = mixed[:, :LANES]
    mixed_ref[1] = mixed[:, LANES:]
    turned = right_ref[2], right_ref[3]
    scale, inverse = scale_ref[0], scale_ref[1]
    for t in range(TOK):
        rotated = dot3(turned, halves(of_token(mixed_ref, t, right_count)), NN)
        bounded = jnp.tanh(rotated * inverse)
        put_token(hold_ref, t, scale * bounded)
        put_token(slope_ref, t, 1.0 - bounded * bounded)
    clip_ref[...] = joined(hold_ref).astype(BF16)


def project_kernel(width, place_ref, clip_ref, own_ref, other_ref, o_ref):
    core = place_ref[0]
    chips = clip_ref.shape[0]
    each = own_ref.shape[0] // width
    total = None
    for ref, base in ((own_ref, core * each), (other_ref, (1 - core) * each)):
        for j in range(each):
            start = pl.multiple_of((base + j) * TOK, TOK)
            part = clip_ref[:, pl.ds(start, TOK), :].reshape(chips * TOK, WIDE)
            term = dot(part[:, :width], ref[j * width : (j + 1) * width, :], NN)
            total = term if total is None else total + term
    o_ref[...] = total.astype(BF16)


def residual_kernel(place_ref, parts_ref, target_hbm, o_ref, rows_ref, sem):
    pair = rows_ref.shape[0]
    start = pl.multiple_of(place_ref[1] * pair, pair)
    copy = pltpu.make_async_copy(target_hbm.at[pl.ds(start, pair)], rows_ref, sem)
    copy.start()
    total = jnp.sum(parts_ref[...].astype(F32), axis=0)
    copy.wait()
    rows = rows_ref[...].astype(F32)
    own = jnp.where(place_ref[2] == 1, rows[TOK:], rows[:TOK])
    grad = (total - own).astype(BF16)
    o_ref[...] = jnp.broadcast_to(grad[None], o_ref.shape)


def back_project_kernel(place_ref, grad_ref, own_ref, other_ref, o_ref):
    step = pl.program_id(0)
    each = pl.num_programs(0) // 2
    core = place_ref[0]
    chips = o_ref.shape[0]

    def put(ref, index):
        part = dot(grad_ref[...], ref[...], NT)
        part = widened(part, part.shape[0]).astype(BF16)
        start = pl.multiple_of(index * TOK, TOK)
        o_ref[:, pl.ds(start, TOK), :] = part.reshape(chips, TOK, WIDE)

    @pl.when(step < each)
    def _():
        put(own_ref, core * each + step)

    @pl.when(step >= each)
    def _():
        put(other_ref, (1 - core) * each + step - each)


def packed_factors(width, grad_left, grad_right):
    low = WIDE - width
    rest = widened(grad_right[2 * low :], grad_right.shape[0] - 2 * low)
    height = rest.shape[0]
    lane = lax.broadcasted_iota(jnp.int32, (height, WIDE), 1)
    pieces = []
    for m in range(width // height):
        top = grad_left[m * height : (m + 1) * height]
        if m * low < grad_right.shape[1]:
            moved = pltpu.roll(rest, width - m * low, axis=1)
            top = jnp.where(lane < width, top, moved)
        pieces.append(top)
    pieces.append(grad_left[width // height * height : width])
    bottom = jnp.concatenate([grad_right[:low], grad_right[low : 2 * low]], axis=1)
    return jnp.concatenate([*pieces, bottom], axis=0)


def backward_kernel(width, grad_ref, slope_ref, mixed_ref, x_ref, right_ref, o_ref, hold_ref, back_ref):
    right_count = right_ref.shape[1]
    owners = o_ref.shape[0]
    own_rows = x_ref.shape[0] // owners
    for side in range(2):
        lanes = slice(side * LANES, (side + 1) * LANES)
        hold_ref[side] = grad_ref[:, lanes].astype(F32) * slope_ref[side]
    right = right_ref[0], right_ref[1]
    grad_right = None
    for t in range(TOK):
        rotated_grad = halves(of_token(hold_ref, t, right_count))
        put_token(back_ref, t, dot3(right, rotated_grad, NN))
        term = dot3(halves(of_token(mixed_ref, t, right_count)), rotated_grad, NT)
        grad_right = term if grad_right is None else grad_right + term
    high, low = halves(joined(back_ref))
    x = x_ref[...]
    grad_left = dot(x, high, TN) + dot(x, low, TN)
    o_ref[:, :own_rows, :] = high.reshape(owners, own_rows, WIDE)
    packed = packed_factors(width, grad_left, grad_right)
    o_ref[:, own_rows:, :] = packed.reshape(owners, TOK, WIDE).astype(BF16)


def input_grad_kernel(width, back_ref, left_ref, o_ref, factor_ref):
    chips, _, total, _ = back_ref.shape
    count = total // TOK - 1
    half = chips * TOK
    left_high, left_low = left_ref[0, :width], left_ref[1, :width]
    for j in range(count):
        for core in range(2):
            part = back_ref[:, core, j * TOK : (j + 1) * TOK, :].reshape(half, WIDE)
            o_ref[j * width : (j + 1) * width, core * half : (core + 1) * half] = dot(
                left_high, part, NT
            ) + dot(left_low, part, NT)
    factors = back_ref[:, :, count * TOK :, :].astype(F32)
    factor_ref[...] = jnp.broadcast_to(jnp.sum(factors, axis=(0, 1))[None], factor_ref.shape)


def sum_and_copy_kernel(parts_ref, o_ref):
    o_ref[...] = jnp.broadcast_to(jnp.sum(parts_ref[...], axis=0)[None], o_ref.shape)


def unpack_kernel(parts_ref, left_ref, right_ref):
    width, count = left_ref.shape[0], right_ref.shape[0]
    packed = parts_ref[...].reshape(WIDE, WIDE)
    left_ref[...] = packed[:width, :width]
    low = WIDE - width
    right_ref[:low, :] = packed[width:, :count]
    right_ref[low : 2 * low, :] = packed[width:, count:]
    height = count - 2 * low
    lane = lax.broadcasted_iota(jnp.int32, (height, WIDE), 1)
    rest = jnp.zeros((height, WIDE), F32)
    for m in range(-(-count // low)):
        back = pltpu.roll(packed[m * height : (m + 1) * height], WIDE - width + m * low, axis=1)
        rest = jnp.where((lane >= m * low) & (lane < (m + 1) * low), back, rest)
    right_ref[2 * low :, :] = rest[:, :count]


def in_hbm(array):
    return pltpu.with_memory_space_constraint(array, HBM)


def exchange(array, axes):
    return lax.all_to_all(array, axes, split_axis=0, concat_axis=0, tiled=True)


def local(activations, left_factor, right_factor, clip_scale, weight_rows, target):
    tokens, hidden = activations.shape
    width, right_count = left_factor.shape[0], right_factor.shape[0]
    columns = weight_rows.shape[1]
    each = hidden // width
    chips = lax.axis_size(CHIPS)
    owners = 2 * chips
    half = tokens // 2
    rows = right_count * TOK
    core = lax.axis_index("core")
    slot = core * chips + lax.axis_index(CHIPS)
    place = jnp.stack([core, slot // 2, slot % 2])

    other_rows = lax.ppermute(weight_rows, "core", [(0, 1), (1, 0)])

    turned_x, turned_scale = activations.T, clip_scale.T
    by_token, left_parts, right_parts, scales = call(
        functools.partial(first_kernel, width),
        (
            shape(chips, 2, each, TOK, WIDE),
            shape(2, WIDE, WIDE),
            shape(4, right_count, right_count),
            shape(2, right_count, WIDE, dtype=F32),
        ),
        "first",
        0,
        4 * tokens * hidden,
        in_specs=[pl.BlockSpec(memory_space=HBM)] * 4,
        scratch_shapes=[
            pltpu.VMEM(turned_x.shape, BF16),
            pltpu.VMEM(left_factor.shape, F32),
            pltpu.VMEM(right_factor.shape, F32),
            pltpu.VMEM(turned_scale.shape, F32),
            pltpu.SemaphoreType.DMA((each // 2 + 3,)),
        ],
    )(*map(in_hbm, (turned_x, left_factor, right_factor, turned_scale)))
    by_token, place = lax.optimization_barrier((by_token, place))
    moved = exchange(by_token.reshape(owners, each * TOK, WIDE), TENSOR).reshape(rows, WIDE)

    lanes_apart = shape(2, rows, LANES, dtype=F32)
    hold = pltpu.VMEM((2, rows, LANES), F32)
    clipped, slope, mixed = call(
        forward_kernel,
        (shape(rows, WIDE), lanes_apart, lanes_apart),
        "forward",
        4 * rows * width * width + 6 * rows * width * right_count,
        12 * rows * width,
        scratch_shapes=[hold],
    )(moved, left_parts, right_parts, scales)
    clipped_back = exchange(clipped.reshape(chips, 2 * each * TOK, WIDE), CHIPS)

    block = 1024
    smem = pl.BlockSpec(memory_space=pltpu.SMEM)
    partial_out = call(
        functools.partial(project_kernel, width),
        shape(half, columns),
        "project",
        4 * half * hidden * columns,
        4 * hidden * columns,
        grid=(columns // block,),
        in_specs=[
            smem,
            pl.BlockSpec((chips, 2 * each * TOK, WIDE), lambda i: (0, 0, 0)),
            pl.BlockSpec((hidden, block), lambda i: (0, i)),
            pl.BlockSpec((hidden, block), lambda i: (0, i)),
        ],
        out_specs=pl.BlockSpec((half, block), lambda i: (0, i)),
    )(place, clipped_back, in_hbm(weight_rows), in_hbm(other_rows))
    arrived = exchange(partial_out.reshape(chips, TOK, columns), CHIPS)

    grad_copies = call(
        residual_kernel,
        shape(chips, TOK, columns),
        "residual",
        0,
        4 * half * columns,
        in_specs=[smem, pl.BlockSpec(), pl.BlockSpec(memory_space=HBM)],
        scratch_shapes=[pltpu.VMEM((2 * TOK, columns), BF16), pltpu.SemaphoreType.DMA(())],
    )(place, arrived, in_hbm(target))
    out_grad = exchange(grad_copies, CHIPS).reshape(half, columns)

    clipped_grad = call(
        back_project_kernel,
        shape(chips, 2 * each * TOK, WIDE),
        "back_project",
        4 * half * hidden * columns,
        4 * hidden * columns,
        grid=(2 * each,),
        in_specs=[
            smem,
            pl.BlockSpec((half, columns), lambda i: (0, 0)),
            pl.BlockSpec((width, columns), lambda i: (jnp.minimum(i, each - 1), 0)),
            pl.BlockSpec((width, columns), lambda i: (jnp.maximum(i - each, 0), 0)),
        ],
        out_specs=pl.BlockSpec((chips, 2 * each * TOK, WIDE), lambda i: (0, 0, 0)),
    )(place, out_grad, weight_rows, other_rows)
    grad_owned = exchange(clipped_grad, CHIPS).reshape(rows, WIDE)

    per_owner = (each + 1) * TOK
    packed = call(
        functools.partial(backward_kernel, width),
        shape(owners, per_owner, WIDE),
        "backward",
        4 * rows * width * width + 12 * rows * width * right_count,
        14 * rows * width,
        scratch_shapes=[hold, hold],
    )(grad_owned, slope, mixed, moved, right_parts)
    back = exchange(packed, TENSOR).reshape(chips, 2, per_owner, WIDE)

    groups = lax.axis_size("dp")
    input_grad, factor_copies = call(
        functools.partial(input_grad_kernel, width),
        (shape(hidden, tokens, dtype=F32), shape(groups, TOK, WIDE, dtype=F32)),
        "input_grad",
        4 * tokens * hidden * width,
        6 * tokens * hidden,
    )(back, left_parts)
    factor_parts = exchange(factor_copies, "dp")
    factor_sums = call(
        sum_and_copy_kernel, shape(owners, TOK, WIDE, dtype=F32), "sum_and_copy", 0, 1 << 20
    )(factor_parts)
    gathered = exchange(factor_sums, TENSOR)
    left_sum, right_sum = call(
        unpack_kernel,
        (shape(width, width, dtype=F32), shape(right_count, right_count, dtype=F32)),
        "unpack",
        0,
        1 << 19,
    )(gathered)
    return left_sum, right_sum, input_grad.T


def solution(mesh):
    torus = Mesh(mesh.devices.reshape(mesh.shape["dp"], 4, 4, 2), ("dp", *TENSOR))
    placed = (P("dp", TENSOR), P(), P(), P(), P(TENSOR, None), P("dp", None))
    return jax.shard_map(
        local, mesh=torus, in_specs=placed, out_specs=(P(), P(), P("dp", TENSOR)), check_vma=False
    )
```

```python
import functools

import jax
import jax.numpy as jnp
from jax import lax
from jax.experimental import pallas as pl
from jax.experimental.pallas import tpu as pltpu
from jax.sharding import Mesh
from jax.sharding import PartitionSpec as P

CHIPS = ("chip_x", "chip_y")
TENSOR = (*CHIPS, "core")
F32, BF16 = jnp.float32, jnp.bfloat16
HBM = pltpu.MemorySpace.HBM
TN = (((0,), (0,)), ((), ()))
NT = (((1,), (1,)), ((), ()))
NN = (((1,), (0,)), ((), ()))

LANES, WIDE = 128, 256
TOK = 8


def call(kernel, outs, name, flops=0, moved=0, vmem=16, **kw):
    return pl.pallas_call(
        kernel,
        out_shape=outs,
        compiler_params=pltpu.CompilerParams(vmem_limit_bytes=vmem << 20),
        cost_estimate=pl.CostEstimate(flops=flops, bytes_accessed=moved, transcendentals=0),
        name=name,
        **kw,
    )


def shape(*lengths, dtype=BF16):
    return jax.ShapeDtypeStruct(lengths, dtype)


def halves(a):
    high = a.astype(BF16)
    return high, (a - high.astype(F32)).astype(BF16)


def dot(a, b, dims):
    return lax.dot_general(a, b, dims, preferred_element_type=F32)


def dot3(a, b, dims):
    (a_high, a_low), (b_high, b_low) = a, b
    return dot(a_high, b_high, dims) + (dot(a_high, b_low, dims) + dot(a_low, b_high, dims))


def of_token(ref, token, count):
    rows = pl.ds(token, count, stride=TOK)
    return jnp.concatenate([ref[0, rows, :], ref[1, rows, :]], axis=1)


def put_token(ref, token, value):
    rows = pl.ds(token, value.shape[0], stride=TOK)
    ref[0, rows, :] = value[:, :LANES]
    ref[1, rows, :] = value[:, LANES:]


def joined(ref):
    return jnp.concatenate([ref[0], ref[1]], axis=1)


def widened(a, rows, value=0.0):
    return jnp.pad(a, ((0, rows - a.shape[0]), (0, WIDE - a.shape[1])), constant_values=value)


def first_kernel(width, *refs):
    *sources, o_ref, left_ref, right_ref, scale_ref = refs[:8]
    *buffers, sems = refs[8:]
    x_hbm, x_buf = sources[0], buffers[0]
    count = x_hbm.shape[0] // width
    tall = 2 * width
    cuts = [pl.ds(i * tall, tall) for i in range(count // 2)]
    pairs = [(x_hbm.at[cut], x_buf.at[cut]) for cut in cuts] + list(zip(sources[1:], buffers[1:]))
    copies = [
        pltpu.make_async_copy(src, dst, sems.at[i]) for i, (src, dst) in enumerate(pairs)
    ]
    for copy in copies:
        copy.start()
    for j in range(count):
        if j % 2 == 0:
            copies[j // 2].wait()
        part = x_buf[j * width : (j + 1) * width, :].astype(F32)
        part = jnp.pad(part, ((0, WIDE - width), (0, 0)))
        turned = part.T.astype(BF16)
        half = turned.shape[0] // 2
        for core in range(2):
            o_ref[:, core, j] = turned[core * half : (core + 1) * half].reshape(-1, TOK, WIDE)
    for copy in copies[count // 2 :]:
        copy.wait()
    _, left_buf, right_buf, scale_buf = buffers
    left_ref[0], left_ref[1] = halves(widened(left_buf[...], WIDE))
    right_ref[0], right_ref[1] = halves(right_buf[...])
    right_ref[2], right_ref[3] = halves(right_buf[...].T)
    scale = widened(scale_buf[...].T, right_buf.shape[0], 1.0)
    scale_ref[0] = scale
    scale_ref[1] = 1.0 / scale


def forward_kernel(place_ref, x_ref, left_ref, right_ref, scale_ref, clip_ref, slope_ref, mixed_ref, hold_ref):
    right_count = right_ref.shape[1]
    x = x_ref[...]
    mixed = dot(x, left_ref[0], NN) + dot(x, left_ref[1], NN)
    mixed_ref[0] = mixed[:, :LANES]
    mixed_ref[1] = mixed[:, LANES:]
    turned = right_ref[2], right_ref[3]
    scale, inverse = scale_ref[0], scale_ref[1]
    for t in range(TOK):
        rotated = dot3(turned, halves(of_token(mixed_ref, t, right_count)), NN)
        bounded = jnp.tanh(rotated * inverse)
        put_token(hold_ref, t, scale * bounded)
        put_token(slope_ref, t, 1.0 - bounded * bounded)
    chips, _, joint = clip_ref.shape
    each = right_count // chips // 2
    width = joint // each // 2
    for chip in range(chips):
        parts = []
        for side in range(2):
            base = chip * 2 * each + lax.rem(place_ref[0] + side, 2) * each
            for j in range(each):
                rows = pl.ds(pl.multiple_of((base + j) * TOK, TOK), TOK)
                parts += [hold_ref[0, rows, :], hold_ref[1, rows, :][:, : width - LANES]]
        clip_ref[chip] = jnp.concatenate(parts, axis=1).astype(BF16)


def project_kernel(clip_ref, own_hbm, other_hbm, o_ref, near_ref, sems):
    chips, _, depth = clip_ref.shape
    hidden, columns = own_hbm.shape
    block = columns // sems.shape[0]
    cuts = [pl.ds(i * block, block) for i in range(sems.shape[0])]
    copies = [
        [
            pltpu.make_async_copy(
                ref.at[:, cut], near_ref.at[pl.ds(side * hidden, hidden), cut], sems.at[i, side]
            )
            for side, ref in enumerate((own_hbm, other_hbm))
        ]
        for i, cut in enumerate(cuts)
    ]
    for pair in copies:
        for copy in pair:
            copy.start()
    part = clip_ref[...].reshape(chips * TOK, depth)
    for cut, pair in zip(cuts, copies):
        for copy in pair:
            copy.wait()
        o_ref[:, cut] = dot(part, near_ref[:, cut], NN).astype(BF16)


def residual_kernel(place_ref, parts_ref, target_hbm, o_ref, rows_ref, sem):
    pair = rows_ref.shape[0]
    start = pl.multiple_of(place_ref[1] * pair, pair)
    copy = pltpu.make_async_copy(target_hbm.at[pl.ds(start, pair)], rows_ref, sem)
    copy.start()
    total = jnp.sum(parts_ref[...].astype(F32), axis=0)
    copy.wait()
    rows = rows_ref[...].astype(F32)
    own = jnp.where(place_ref[2] == 1, rows[TOK:], rows[:TOK])
    grad = (total - own).astype(BF16)
    o_ref[...] = jnp.broadcast_to(grad[None], o_ref.shape)


def packed_factors(width, grad_left, grad_right):
    low = WIDE - width
    rest = widened(grad_right[2 * low :], grad_right.shape[0] - 2 * low)
    height = rest.shape[0]
    lane = lax.broadcasted_iota(jnp.int32, (height, WIDE), 1)
    pieces = []
    for m in range(width // height):
        top = grad_left[m * height : (m + 1) * height]
        if m * low < grad_right.shape[1]:
            moved = pltpu.roll(rest, width - m * low, axis=1)
            top = jnp.where(lane < width, top, moved)
        pieces.append(top)
    pieces.append(grad_left[width // height * height : width])
    bottom = jnp.concatenate([grad_right[:low], grad_right[low : 2 * low]], axis=1)
    return jnp.concatenate([*pieces, bottom], axis=0)


def backward_kernel(width, place_ref, grad_ref, slope_ref, mixed_ref, x_ref, right_ref, o_ref, hold_ref, back_ref):
    right_count = right_ref.shape[1]
    owners = o_ref.shape[0]
    own_rows = x_ref.shape[0] // owners
    chips, _, joint = grad_ref.shape
    each = joint // width // 2
    for chip in range(chips):
        rows_of_chip = grad_ref[chip].astype(F32)
        for side in range(2):
            base = chip * 2 * each + lax.rem(place_ref[0] + side, 2) * each
            for j in range(each):
                rows = pl.ds(pl.multiple_of((base + j) * TOK, TOK), TOK)
                start = (side * each + j) * width
                part = widened(rows_of_chip[:, start : start + width], TOK)
                hold_ref[0, rows, :] = part[:, :LANES] * slope_ref[0, rows, :]
                hold_ref[1, rows, :] = part[:, LANES:] * slope_ref[1, rows, :]
    right = right_ref[0], right_ref[1]
    grad_right = None
    for t in range(TOK):
        rotated_grad = halves(of_token(hold_ref, t, right_count))
        put_token(back_ref, t, dot3(right, rotated_grad, NN))
        term = dot3(halves(of_token(mixed_ref, t, right_count)), rotated_grad, NT)
        grad_right = term if grad_right is None else grad_right + term
    high, low = halves(joined(back_ref))
    x = x_ref[...]
    grad_left = dot(x, high, TN) + dot(x, low, TN)
    o_ref[:, :own_rows, :] = high.reshape(owners, own_rows, WIDE)
    packed = packed_factors(width, grad_left, grad_right)
    o_ref[:, own_rows:, :] = packed.reshape(owners, TOK, WIDE).astype(BF16)


def input_grad_kernel(width, back_ref, left_ref, o_ref, factor_ref):
    chips, _, total, _ = back_ref.shape
    count = total // TOK - 1
    half = chips * TOK
    left_high, left_low = left_ref[0, :width], left_ref[1, :width]
    for j in range(count):
        for core in range(2):
            part = back_ref[:, core, j * TOK : (j + 1) * TOK, :].reshape(half, WIDE)
            o_ref[j * width : (j + 1) * width, core * half : (core + 1) * half] = dot(
                left_high, part, NT
            ) + dot(left_low, part, NT)
    factors = back_ref[:, :, count * TOK :, :].astype(F32)
    factor_ref[...] = jnp.broadcast_to(jnp.sum(factors, axis=(0, 1))[None], factor_ref.shape)


def sum_and_copy_kernel(parts_ref, o_ref):
    o_ref[...] = jnp.broadcast_to(jnp.sum(parts_ref[...], axis=0)[None], o_ref.shape)


def unpack_kernel(parts_ref, left_ref, right_ref):
    width, count = left_ref.shape[0], right_ref.shape[0]
    packed = parts_ref[...].reshape(WIDE, WIDE)
    left_ref[...] = packed[:width, :width]
    low = WIDE - width
    right_ref[:low, :] = packed[width:, :count]
    right_ref[low : 2 * low, :] = packed[width:, count:]
    height = count - 2 * low
    lane = lax.broadcasted_iota(jnp.int32, (height, WIDE), 1)
    rest = jnp.zeros((height, WIDE), F32)
    for m in range(-(-count // low)):
        back = pltpu.roll(packed[m * height : (m + 1) * height], WIDE - width + m * low, axis=1)
        rest = jnp.where((lane >= m * low) & (lane < (m + 1) * low), back, rest)
    right_ref[2 * low :, :] = rest[:, :count]


def in_hbm(array):
    return pltpu.with_memory_space_constraint(array, HBM)


def exchange(array, axes):
    return lax.all_to_all(array, axes, split_axis=0, concat_axis=0, tiled=True)


def local(activations, left_factor, right_factor, clip_scale, weight_rows, target):
    tokens, hidden = activations.shape
    width, right_count = left_factor.shape[0], right_factor.shape[0]
    columns = weight_rows.shape[1]
    each = hidden // width
    chips = lax.axis_size(CHIPS)
    owners = 2 * chips
    half = tokens // 2
    rows = right_count * TOK
    core = lax.axis_index("core")
    smem = pl.BlockSpec(memory_space=pltpu.SMEM)
    slot = core * chips + lax.axis_index(CHIPS)
    place = jnp.stack([core, slot // 2, slot % 2])

    other_rows = lax.ppermute(weight_rows, "core", [(0, 1), (1, 0)])

    turned_x, turned_scale = activations.T, clip_scale.T
    by_token, left_parts, right_parts, scales = call(
        functools.partial(first_kernel, width),
        (
            shape(chips, 2, each, TOK, WIDE),
            shape(2, WIDE, WIDE),
            shape(4, right_count, right_count),
            shape(2, right_count, WIDE, dtype=F32),
        ),
        "first",
        0,
        4 * tokens * hidden,
        in_specs=[pl.BlockSpec(memory_space=HBM)] * 4,
        scratch_shapes=[
            pltpu.VMEM(turned_x.shape, BF16),
            pltpu.VMEM(left_factor.shape, F32),
            pltpu.VMEM(right_factor.shape, F32),
            pltpu.VMEM(turned_scale.shape, F32),
            pltpu.SemaphoreType.DMA((each // 2 + 3,)),
        ],
    )(*map(in_hbm, (turned_x, left_factor, right_factor, turned_scale)))
    by_token, place = lax.optimization_barrier((by_token, place))
    moved = exchange(by_token.reshape(owners, each * TOK, WIDE), TENSOR).reshape(rows, WIDE)

    lanes_apart = shape(2, rows, LANES, dtype=F32)
    hold = pltpu.VMEM((2, rows, LANES), F32)
    clipped, slope, mixed = call(
        forward_kernel,
        (shape(chips, TOK, 2 * hidden), lanes_apart, lanes_apart),
        "forward",
        4 * rows * width * width + 6 * rows * width * right_count,
        12 * rows * width,
        in_specs=[smem, *[pl.BlockSpec()] * 4],
        scratch_shapes=[hold],
    )(place, moved, left_parts, right_parts, scales)
    clipped_back = exchange(clipped, CHIPS)
    partial_out, near_rows = call(
        project_kernel,
        (shape(half, columns), shape(2 * hidden, columns)),
        "project",
        4 * half * hidden * columns,
        4 * hidden * columns,
        vmem=24,
        in_specs=[pl.BlockSpec(), *[pl.BlockSpec(memory_space=HBM)] * 2],
        scratch_shapes=[pltpu.SemaphoreType.DMA((5, 2))],
    )(clipped_back, in_hbm(weight_rows), in_hbm(other_rows))
    arrived = exchange(partial_out.reshape(chips, TOK, columns), CHIPS)

    grad_copies = call(
        residual_kernel,
        shape(chips, TOK, columns),
        "residual",
        0,
        4 * half * columns,
        in_specs=[smem, pl.BlockSpec(), pl.BlockSpec(memory_space=HBM)],
        scratch_shapes=[pltpu.VMEM((2 * TOK, columns), BF16), pltpu.SemaphoreType.DMA(())],
    )(place, arrived, in_hbm(target))
    out_grad = exchange(grad_copies, CHIPS).reshape(half, columns)

    clipped_grad = dot(out_grad, near_rows, NT).astype(BF16)
    grad_owned = exchange(clipped_grad.reshape(chips, TOK, 2 * hidden), CHIPS)

    per_owner = (each + 1) * TOK
    packed = call(
        functools.partial(backward_kernel, width),
        shape(owners, per_owner, WIDE),
        "backward",
        4 * rows * width * width + 12 * rows * width * right_count,
        14 * rows * width,
        in_specs=[smem, *[pl.BlockSpec()] * 5],
        scratch_shapes=[hold, hold],
    )(place, grad_owned, slope, mixed, moved, right_parts)
    back = exchange(packed, TENSOR).reshape(chips, 2, per_owner, WIDE)

    groups = lax.axis_size("dp")
    input_grad, factor_copies = call(
        functools.partial(input_grad_kernel, width),
        (shape(hidden, tokens, dtype=F32), shape(groups, TOK, WIDE, dtype=F32)),
        "input_grad",
        4 * tokens * hidden * width,
        6 * tokens * hidden,
    )(back, left_parts)
    factor_parts = exchange(factor_copies, "dp")
    factor_sums = call(
        sum_and_copy_kernel, shape(owners, TOK, WIDE, dtype=F32), "sum_and_copy", 0, 1 << 20
    )(factor_parts)
    gathered = exchange(factor_sums, TENSOR)
    left_sum, right_sum = call(
        unpack_kernel,
        (shape(width, width, dtype=F32), shape(right_count, right_count, dtype=F32)),
        "unpack",
        0,
        1 << 19,
    )(gathered)
    return left_sum, right_sum, input_grad.T


def solution(mesh):
    torus = Mesh(mesh.devices.reshape(mesh.shape["dp"], 4, 4, 2), ("dp", *TENSOR))
    placed = (P("dp", TENSOR), P(), P(), P(), P(TENSOR, None), P("dp", None))
    return jax.shard_map(
        local, mesh=torus, in_specs=placed, out_specs=(P(), P(), P("dp", TENSOR)), check_vma=False
    )
```

```python
import functools

import jax
import jax.numpy as jnp
from jax import lax
from jax.experimental import pallas as pl
from jax.experimental.pallas import tpu as pltpu
from jax.sharding import Mesh
from jax.sharding import PartitionSpec as P

CHIPS = ("chip_x", "chip_y")
TENSOR = (*CHIPS, "core")
F32, BF16 = jnp.float32, jnp.bfloat16
HBM = pltpu.MemorySpace.HBM
TN = (((0,), (0,)), ((), ()))
NT = (((1,), (1,)), ((), ()))
NN = (((1,), (0,)), ((), ()))

LANES, WIDE = 128, 256
TOK = 8


def call(kernel, outs, name, flops=0, moved=0, vmem=16, **kw):
    return pl.pallas_call(
        kernel,
        out_shape=outs,
        compiler_params=pltpu.CompilerParams(vmem_limit_bytes=vmem << 20),
        cost_estimate=pl.CostEstimate(flops=flops, bytes_accessed=moved, transcendentals=0),
        name=name,
        **kw,
    )


def shape(*lengths, dtype=BF16):
    return jax.ShapeDtypeStruct(lengths, dtype)


def halves(a):
    high = a.astype(BF16)
    return high, (a - high.astype(F32)).astype(BF16)


def dot(a, b, dims):
    return lax.dot_general(a, b, dims, preferred_element_type=F32)


def dot3(a, b, dims):
    (a_high, a_low), (b_high, b_low) = a, b
    return dot(a_high, b_high, dims) + (dot(a_high, b_low, dims) + dot(a_low, b_high, dims))


def of_token(ref, token, count):
    rows = pl.ds(token, count, stride=TOK)
    return jnp.concatenate([ref[0, rows, :], ref[1, rows, :]], axis=1)


def put_token(ref, token, value):
    rows = pl.ds(token, value.shape[0], stride=TOK)
    ref[0, rows, :] = value[:, :LANES]
    ref[1, rows, :] = value[:, LANES:]


def joined(ref):
    return jnp.concatenate([ref[0], ref[1]], axis=1)


def widened(a, rows, value=0.0):
    return jnp.pad(a, ((0, rows - a.shape[0]), (0, WIDE - a.shape[1])), constant_values=value)


def first_kernel(width, *refs):
    *sources, o_ref, left_ref, right_ref, scale_ref = refs[:8]
    *buffers, sems = refs[8:]
    x_hbm, x_buf = sources[0], buffers[0]
    count = x_hbm.shape[0] // width
    tall = 2 * width
    cuts = [pl.ds(i * tall, tall) for i in range(count // 2)]
    pairs = [(x_hbm.at[cut], x_buf.at[cut]) for cut in cuts] + list(zip(sources[1:], buffers[1:]))
    copies = [
        pltpu.make_async_copy(src, dst, sems.at[i]) for i, (src, dst) in enumerate(pairs)
    ]
    for copy in copies:
        copy.start()
    for j in range(count):
        if j % 2 == 0:
            copies[j // 2].wait()
        part = x_buf[j * width : (j + 1) * width, :].astype(F32)
        part = jnp.pad(part, ((0, WIDE - width), (0, 0)))
        turned = part.T.astype(BF16)
        half = turned.shape[0] // 2
        for core in range(2):
            o_ref[:, core, j] = turned[core * half : (core + 1) * half].reshape(-1, TOK, WIDE)
    for copy in copies[count // 2 :]:
        copy.wait()
    _, left_buf, right_buf, scale_buf = buffers
    left_ref[0], left_ref[1] = halves(widened(left_buf[...], WIDE))
    right_ref[0], right_ref[1] = halves(right_buf[...])
    right_ref[2], right_ref[3] = halves(right_buf[...].T)
    scale = widened(scale_buf[...].T, right_buf.shape[0], 1.0)
    scale_ref[0] = scale
    scale_ref[1] = 1.0 / scale


def forward_kernel(place_ref, x_ref, left_ref, right_ref, scale_ref, clip_ref, slope_ref, mixed_ref, hold_ref):
    right_count = right_ref.shape[1]
    x = x_ref[...]
    mixed = dot(x, left_ref[0], NN) + dot(x, left_ref[1], NN)
    mixed_ref[0] = mixed[:, :LANES]
    mixed_ref[1] = mixed[:, LANES:]
    turned = right_ref[2], right_ref[3]
    scale, inverse = scale_ref[0], scale_ref[1]
    for t in range(TOK):
        rotated = dot3(turned, halves(of_token(mixed_ref, t, right_count)), NN)
        bounded = jnp.tanh(rotated * inverse)
        put_token(hold_ref, t, scale * bounded)
        put_token(slope_ref, t, 1.0 - bounded * bounded)
    chips, _, joint = clip_ref.shape
    each = right_count // chips // 2
    width = joint // each // 2
    for chip in range(chips):
        parts = []
        for side in range(2):
            base = chip * 2 * each + lax.rem(place_ref[0] + side, 2) * each
            for j in range(each):
                rows = pl.ds(pl.multiple_of((base + j) * TOK, TOK), TOK)
                parts += [hold_ref[0, rows, :], hold_ref[1, rows, :][:, : width - LANES]]
        clip_ref[chip] = jnp.concatenate(parts, axis=1).astype(BF16)


def project_kernel(clip_ref, own_hbm, other_hbm, o_ref, near_ref, sems):
    chips, _, depth = clip_ref.shape
    hidden, columns = own_hbm.shape
    block = columns // sems.shape[0]
    cuts = [pl.ds(i * block, block) for i in range(sems.shape[0])]
    copies = [
        [
            pltpu.make_async_copy(
                ref.at[:, cut], near_ref.at[pl.ds(side * hidden, hidden), cut], sems.at[i, side]
            )
            for side, ref in enumerate((own_hbm, other_hbm))
        ]
        for i, cut in enumerate(cuts)
    ]
    for pair in copies:
        for copy in pair:
            copy.start()
    part = clip_ref[...].reshape(chips * TOK, depth)
    for cut, pair in zip(cuts, copies):
        for copy in pair:
            copy.wait()
        o_ref[:, cut] = dot(part, near_ref[:, cut], NN).astype(BF16)


def residual_kernel(place_ref, parts_ref, target_hbm, o_ref, rows_ref, sem):
    pair = rows_ref.shape[0]
    start = pl.multiple_of(place_ref[1] * pair, pair)
    copy = pltpu.make_async_copy(target_hbm.at[pl.ds(start, pair)], rows_ref, sem)
    copy.start()
    total = jnp.sum(parts_ref[...].astype(F32), axis=0)
    copy.wait()
    rows = rows_ref[...].astype(F32)
    own = jnp.where(place_ref[2] == 1, rows[TOK:], rows[:TOK])
    grad = (total - own).astype(BF16)
    o_ref[...] = jnp.broadcast_to(grad[None], o_ref.shape)


def turn_kernel(x_ref, o_ref):
    o_ref[...] = x_ref[...].T


def packed_factors(width, grad_left, grad_right):
    low = WIDE - width
    rest = widened(grad_right[2 * low :], grad_right.shape[0] - 2 * low)
    height = rest.shape[0]
    lane = lax.broadcasted_iota(jnp.int32, (height, WIDE), 1)
    pieces = []
    for m in range(width // height):
        top = grad_left[m * height : (m + 1) * height]
        if m * low < grad_right.shape[1]:
            moved = pltpu.roll(rest, width - m * low, axis=1)
            top = jnp.where(lane < width, top, moved)
        pieces.append(top)
    pieces.append(grad_left[width // height * height : width])
    bottom = jnp.concatenate([grad_right[:low], grad_right[low : 2 * low]], axis=1)
    return jnp.concatenate([*pieces, bottom], axis=0)


def backward_kernel(width, place_ref, grad_ref, slope_ref, mixed_ref, x_ref, right_ref, o_ref, hold_ref, back_ref):
    right_count = right_ref.shape[1]
    owners = o_ref.shape[0]
    own_rows = x_ref.shape[0] // owners
    chips, _, joint = grad_ref.shape
    each = joint // width // 2
    for chip in range(chips):
        rows_of_chip = grad_ref[chip].astype(F32)
        for side in range(2):
            base = chip * 2 * each + lax.rem(place_ref[0] + side, 2) * each
            for j in range(each):
                rows = pl.ds(pl.multiple_of((base + j) * TOK, TOK), TOK)
                start = (side * each + j) * width
                part = widened(rows_of_chip[:, start : start + width], TOK)
                hold_ref[0, rows, :] = part[:, :LANES] * slope_ref[0, rows, :]
                hold_ref[1, rows, :] = part[:, LANES:] * slope_ref[1, rows, :]
    right = right_ref[0], right_ref[1]
    grad_right = None
    for t in range(TOK):
        rotated_grad = halves(of_token(hold_ref, t, right_count))
        put_token(back_ref, t, dot3(right, rotated_grad, NN))
        term = dot3(halves(of_token(mixed_ref, t, right_count)), rotated_grad, NT)
        grad_right = term if grad_right is None else grad_right + term
    high, low = halves(joined(back_ref))
    x = x_ref[...]
    grad_left = dot(x, high, TN) + dot(x, low, TN)
    o_ref[:, :own_rows, :] = high.reshape(owners, own_rows, WIDE)
    packed = packed_factors(width, grad_left, grad_right)
    o_ref[:, own_rows:, :] = packed.reshape(owners, TOK, WIDE).astype(BF16)


def input_grad_kernel(width, back_ref, left_ref, o_ref, factor_ref):
    chips, _, total, _ = back_ref.shape
    count = total // TOK - 1
    half = chips * TOK
    left_high, left_low = left_ref[0, :width], left_ref[1, :width]
    for j in range(count):
        for core in range(2):
            part = back_ref[:, core, j * TOK : (j + 1) * TOK, :].reshape(half, WIDE)
            o_ref[j * width : (j + 1) * width, core * half : (core + 1) * half] = dot(
                left_high, part, NT
            ) + dot(left_low, part, NT)
    factors = back_ref[:, :, count * TOK :, :].astype(F32)
    factor_ref[...] = jnp.broadcast_to(jnp.sum(factors, axis=(0, 1))[None], factor_ref.shape)


def sum_and_copy_kernel(parts_ref, o_ref):
    o_ref[...] = jnp.broadcast_to(jnp.sum(parts_ref[...], axis=0)[None], o_ref.shape)


def unpack_kernel(parts_ref, left_ref, right_ref):
    width, count = left_ref.shape[0], right_ref.shape[0]
    packed = parts_ref[...].reshape(WIDE, WIDE)
    left_ref[...] = packed[:width, :width]
    low = WIDE - width
    right_ref[:low, :] = packed[width:, :count]
    right_ref[low : 2 * low, :] = packed[width:, count:]
    height = count - 2 * low
    lane = lax.broadcasted_iota(jnp.int32, (height, WIDE), 1)
    rest = jnp.zeros((height, WIDE), F32)
    for m in range(-(-count // low)):
        back = pltpu.roll(packed[m * height : (m + 1) * height], WIDE - width + m * low, axis=1)
        rest = jnp.where((lane >= m * low) & (lane < (m + 1) * low), back, rest)
    right_ref[2 * low :, :] = rest[:, :count]


def in_hbm(array):
    return pltpu.with_memory_space_constraint(array, HBM)


def exchange(array, axes):
    return lax.all_to_all(array, axes, split_axis=0, concat_axis=0, tiled=True)


def local(activations, left_factor, right_factor, clip_scale, weight_rows, target):
    tokens, hidden = activations.shape
    width, right_count = left_factor.shape[0], right_factor.shape[0]
    columns = weight_rows.shape[1]
    each = hidden // width
    chips = lax.axis_size(CHIPS)
    owners = 2 * chips
    half = tokens // 2
    rows = right_count * TOK
    core = lax.axis_index("core")
    smem = pl.BlockSpec(memory_space=pltpu.SMEM)
    slot = core * chips + lax.axis_index(CHIPS)
    place = jnp.stack([core, slot // 2, slot % 2])

    other_rows = lax.ppermute(weight_rows, "core", [(0, 1), (1, 0)])

    turned_x, turned_scale = activations.T, clip_scale.T
    by_token, left_parts, right_parts, scales = call(
        functools.partial(first_kernel, width),
        (
            shape(chips, 2, each, TOK, WIDE),
            shape(2, WIDE, WIDE),
            shape(4, right_count, right_count),
            shape(2, right_count, WIDE, dtype=F32),
        ),
        "first",
        0,
        4 * tokens * hidden,
        in_specs=[pl.BlockSpec(memory_space=HBM)] * 4,
        scratch_shapes=[
            pltpu.VMEM(turned_x.shape, BF16),
            pltpu.VMEM(left_factor.shape, F32),
            pltpu.VMEM(right_factor.shape, F32),
            pltpu.VMEM(turned_scale.shape, F32),
            pltpu.SemaphoreType.DMA((each // 2 + 3,)),
        ],
    )(*map(in_hbm, (turned_x, left_factor, right_factor, turned_scale)))
    by_token, place = lax.optimization_barrier((by_token, place))
    moved = exchange(by_token.reshape(owners, each * TOK, WIDE), TENSOR).reshape(rows, WIDE)

    moved, other_rows = lax.optimization_barrier((moved, other_rows))
    lanes_apart = shape(2, rows, LANES, dtype=F32)
    hold = pltpu.VMEM((2, rows, LANES), F32)
    clipped, slope, mixed = call(
        forward_kernel,
        (shape(chips, TOK, 2 * hidden), lanes_apart, lanes_apart),
        "forward",
        10**10,
        12 * rows * width,
        in_specs=[smem, *[pl.BlockSpec()] * 4],
        scratch_shapes=[hold],
    )(place, moved, left_parts, right_parts, scales)
    clipped_back = exchange(clipped, CHIPS)
    partial_out, near_rows = call(
        project_kernel,
        (shape(half, columns), shape(2 * hidden, columns)),
        "project",
        4 * half * hidden * columns,
        4 * hidden * columns,
        vmem=24,
        in_specs=[pl.BlockSpec(), *[pl.BlockSpec(memory_space=pl.ANY)] * 2],
        scratch_shapes=[pltpu.SemaphoreType.DMA((5, 2))],
    )(clipped_back, weight_rows, in_hbm(other_rows))
    arrived = exchange(partial_out.reshape(chips, TOK, columns), CHIPS)

    grad_copies = call(
        residual_kernel,
        shape(chips, TOK, columns),
        "residual",
        0,
        4 * half * columns,
        in_specs=[smem, pl.BlockSpec(), pl.BlockSpec(memory_space=HBM)],
        scratch_shapes=[pltpu.VMEM((2 * TOK, columns), BF16), pltpu.SemaphoreType.DMA(())],
    )(place, arrived, in_hbm(target))
    out_grad = exchange(grad_copies, CHIPS).reshape(half, columns)

    turned_grad = dot(near_rows, out_grad, NT).astype(BF16)
    clipped_grad = call(
        turn_kernel, shape(half, 2 * hidden), "turn", 0, 8 * half * hidden
    )(turned_grad)
    grad_owned = exchange(clipped_grad.reshape(chips, TOK, 2 * hidden), CHIPS)

    per_owner = (each + 1) * TOK
    packed = call(
        functools.partial(backward_kernel, width),
        shape(owners, per_owner, WIDE),
        "backward",
        4 * rows * width * width + 12 * rows * width * right_count,
        14 * rows * width,
        in_specs=[smem, *[pl.BlockSpec()] * 5],
        scratch_shapes=[hold, hold],
    )(place, grad_owned, slope, mixed, moved, right_parts)
    back = exchange(packed, TENSOR).reshape(chips, 2, per_owner, WIDE)

    groups = lax.axis_size("dp")
    input_grad, factor_copies = call(
        functools.partial(input_grad_kernel, width),
        (shape(hidden, tokens, dtype=F32), shape(groups, TOK, WIDE, dtype=F32)),
        "input_grad",
        4 * tokens * hidden * width,
        6 * tokens * hidden,
    )(back, left_parts)
    factor_parts = exchange(factor_copies, "dp")
    factor_sums = call(
        sum_and_copy_kernel, shape(owners, TOK, WIDE, dtype=F32), "sum_and_copy", 0, 1 << 20
    )(factor_parts)
    gathered = exchange(factor_sums, TENSOR)
    left_sum, right_sum = call(
        unpack_kernel,
        (shape(width, width, dtype=F32), shape(right_count, right_count, dtype=F32)),
        "unpack",
        0,
        1 << 19,
    )(gathered)
    return left_sum, right_sum, input_grad.T


def solution(mesh):
    torus = Mesh(mesh.devices.reshape(mesh.shape["dp"], 4, 4, 2), ("dp", *TENSOR))
    placed = (P("dp", TENSOR), P(), P(), P(), P(TENSOR, None), P("dp", None))
    return jax.shard_map(
        local, mesh=torus, in_specs=placed, out_specs=(P(), P(), P("dp", TENSOR)), check_vma=False
    )
```

```python
import functools

import jax
import jax.numpy as jnp
from jax import lax
from jax.experimental import pallas as pl
from jax.experimental.pallas import tpu as pltpu
from jax.sharding import Mesh
from jax.sharding import PartitionSpec as P

CHIPS = ("chip_x", "chip_y")
TENSOR = (*CHIPS, "core")
F32, BF16 = jnp.float32, jnp.bfloat16
HBM = pltpu.MemorySpace.HBM
TN = (((0,), (0,)), ((), ()))
NT = (((1,), (1,)), ((), ()))
NN = (((1,), (0,)), ((), ()))

LANES, WIDE = 128, 256
TOK = 8


def call(kernel, outs, name, flops=0, moved=0, vmem=16, **kw):
    return pl.pallas_call(
        kernel,
        out_shape=outs,
        compiler_params=pltpu.CompilerParams(vmem_limit_bytes=vmem << 20),
        cost_estimate=pl.CostEstimate(flops=flops, bytes_accessed=moved, transcendentals=0),
        name=name,
        **kw,
    )


def shape(*lengths, dtype=BF16):
    return jax.ShapeDtypeStruct(lengths, dtype)


def halves(a):
    high = a.astype(BF16)
    return high, (a - high.astype(F32)).astype(BF16)


def dot(a, b, dims):
    return lax.dot_general(a, b, dims, preferred_element_type=F32)


def stacked_dot(a, b):
    high, low = b
    count = a.shape[0] // 2
    both = dot(a, high, NN)
    return both[:count] + (both[count:] + dot(a[:count], low, NN))


def of_token(ref, token, count):
    rows = pl.ds(token, count, stride=TOK)
    return jnp.concatenate([ref[0, rows, :], ref[1, rows, :]], axis=1)


def put_token(ref, token, value):
    rows = pl.ds(token, value.shape[0], stride=TOK)
    ref[0, rows, :] = value[:, :LANES]
    ref[1, rows, :] = value[:, LANES:]


def joined(ref):
    return jnp.concatenate([ref[0], ref[1]], axis=1)


def widened(a, rows, value=0.0):
    return jnp.pad(a, ((0, rows - a.shape[0]), (0, WIDE - a.shape[1])), constant_values=value)


def first_kernel(width, *refs):
    *sources, o_ref, left_ref, back_left_ref, right_ref, scale_ref = refs[:9]
    *buffers, sems = refs[9:]
    x_hbm, x_buf = sources[0], buffers[0]
    count = x_hbm.shape[0] // width
    tall = 2 * width
    cuts = [pl.ds(i * tall, tall) for i in range(count // 2)]
    pairs = [(x_hbm.at[cut], x_buf.at[cut]) for cut in cuts] + list(zip(sources[1:], buffers[1:]))
    copies = [
        pltpu.make_async_copy(src, dst, sems.at[i]) for i, (src, dst) in enumerate(pairs)
    ]
    for copy in copies:
        copy.start()
    for j in range(count):
        if j % 2 == 0:
            copies[j // 2].wait()
        part = x_buf[j * width : (j + 1) * width, :].astype(F32)
        part = jnp.pad(part, ((0, WIDE - width), (0, 0)))
        turned = part.T.astype(BF16)
        half = turned.shape[0] // 2
        for core in range(2):
            o_ref[:, core, j] = turned[core * half : (core + 1) * half].reshape(-1, TOK, WIDE)
    for copy in copies[count // 2 :]:
        copy.wait()
    _, left_buf, right_buf, scale_buf = buffers
    high, low = halves(widened(left_buf[...], WIDE))
    left_ref[:, :WIDE] = high
    left_ref[:, WIDE:] = low
    back_left_ref[...] = jnp.concatenate([high[:width], low[:width]], axis=0)
    right_ref[0] = jnp.concatenate(halves(right_buf[...]), axis=0)
    right_ref[1] = jnp.concatenate(halves(right_buf[...].T), axis=0)
    scale = widened(scale_buf[...].T, right_buf.shape[0], 1.0)
    scale_ref[0] = scale
    scale_ref[1] = 1.0 / scale


def forward_kernel(x_ref, left_ref, right_ref, scale_ref, clip_ref, slope_ref, mixed_ref, hold_ref):
    right_count = right_ref.shape[2]
    both = dot(x_ref[...], left_ref[...], NN)
    mixed = both[:, :WIDE] + both[:, WIDE:]
    mixed_ref[0] = mixed[:, :LANES]
    mixed_ref[1] = mixed[:, LANES:]
    turned = right_ref[1]
    scale, inverse = scale_ref[0], scale_ref[1]
    for t in range(TOK):
        rotated = stacked_dot(turned, halves(of_token(mixed_ref, t, right_count)))
        bounded = jnp.tanh(rotated * inverse)
        put_token(hold_ref, t, scale * bounded)
        put_token(slope_ref, t, 1.0 - bounded * bounded)
    core = lax.axis_index("core")
    chips, _, joint = clip_ref.shape
    each = right_count // chips // 2
    width = joint // each // 2
    for chip in range(chips):
        parts = []
        for side in range(2):
            base = chip * 2 * each + lax.rem(core + side, 2) * each
            for j in range(each):
                rows = pl.ds(pl.multiple_of((base + j) * TOK, TOK), TOK)
                parts += [hold_ref[0, rows, :], hold_ref[1, rows, :][:, : width - LANES]]
        clip_ref[chip] = jnp.concatenate(parts, axis=1).astype(BF16)


def own_slot(chips):
    x, y = (lax.axis_index(axis) for axis in CHIPS)
    return lax.axis_index("core") * chips + x * lax.axis_size(CHIPS[1]) + y


def project_kernel(clip_ref, own_ref, other_ref, target_hbm, o_ref, rows_ref, sem):
    chips, _, depth = clip_ref.shape
    hidden, columns = own_ref.shape
    pair = rows_ref.shape[0]
    start = pl.multiple_of(own_slot(chips) // 2 * pair, pair)
    copy = pltpu.make_async_copy(target_hbm.at[pl.ds(start, pair)], rows_ref, sem)
    copy.start()
    part = clip_ref[...].reshape(chips * TOK, depth)
    own, other = part[:, :hidden], part[:, hidden:]
    block = 1024
    for i in range(columns // block):
        cut = slice(i * block, (i + 1) * block)
        total = dot(own, own_ref[:, cut], NN) + dot(other, other_ref[:, cut], NN)
        o_ref[:, cut] = total.astype(BF16)
    copy.wait()


def residual_kernel(parts_ref, rows_ref, o_ref):
    total = jnp.sum(parts_ref[...].astype(F32), axis=0)
    rows = rows_ref[...].astype(F32)
    odd = lax.rem(own_slot(parts_ref.shape[0]), 2) == 1
    own = jnp.where(odd, rows[TOK:], rows[:TOK])
    o_ref[...] = jnp.broadcast_to((total - own).astype(BF16)[None], o_ref.shape)


def turn_kernel(own_ref, other_ref, o_ref):
    hidden = own_ref.shape[0]
    o_ref[:, :hidden] = own_ref[...].T
    o_ref[:, hidden:] = other_ref[...].T


def packed_factors(width, grad_left, grad_right):
    low = WIDE - width
    rest = widened(grad_right[2 * low :], grad_right.shape[0] - 2 * low)
    height = rest.shape[0]
    lane = lax.broadcasted_iota(jnp.int32, (height, WIDE), 1)
    pieces = []
    for m in range(width // height):
        top = grad_left[m * height : (m + 1) * height]
        if m * low < grad_right.shape[1]:
            moved = pltpu.roll(rest, width - m * low, axis=1)
            top = jnp.where(lane < width, top, moved)
        pieces.append(top)
    pieces.append(grad_left[width // height * height : width])
    bottom = jnp.concatenate([grad_right[:low], grad_right[low : 2 * low]], axis=1)
    return jnp.concatenate([*pieces, bottom], axis=0)


def backward_kernel(width, grad_ref, slope_ref, mixed_ref, x_ref, right_ref, o_ref, hold_ref, back_ref):
    right_count = right_ref.shape[2]
    owners = o_ref.shape[0]
    own_rows = x_ref.shape[0] // owners
    core = lax.axis_index("core")
    chips, _, joint = grad_ref.shape
    each = joint // width // 2
    for chip in range(chips):
        rows_of_chip = grad_ref[chip].astype(F32)
        for side in range(2):
            base = chip * 2 * each + lax.rem(core + side, 2) * each
            for j in range(each):
                rows = pl.ds(pl.multiple_of((base + j) * TOK, TOK), TOK)
                start = (side * each + j) * width
                part = widened(rows_of_chip[:, start : start + width], TOK)
                hold_ref[0, rows, :] = part[:, :LANES] * slope_ref[0, rows, :]
                hold_ref[1, rows, :] = part[:, LANES:] * slope_ref[1, rows, :]
    right = right_ref[0]
    grad_right = None
    for t in range(TOK):
        rotated_grad = halves(of_token(hold_ref, t, right_count))
        put_token(back_ref, t, stacked_dot(right, rotated_grad))
        term = dot(of_token(mixed_ref, t, right_count).astype(BF16), rotated_grad[0], NT)
        grad_right = term if grad_right is None else grad_right + term
    mixed_grad = joined(back_ref).astype(BF16)
    grad_left = dot(x_ref[...], mixed_grad, TN)
    o_ref[:, :own_rows, :] = mixed_grad.reshape(owners, own_rows, WIDE)
    packed = packed_factors(width, grad_left, grad_right)
    o_ref[:, own_rows:, :] = packed.reshape(owners, TOK, WIDE).astype(BF16)


def input_grad_kernel(width, back_ref, left_ref, o_hbm, factor_ref, o_ref, sems):
    chips, _, total, _ = back_ref.shape
    count = total // TOK - 1
    half = chips * TOK
    copies = []
    for j in range(count):
        parts = [
            back_ref[:, core, j * TOK : (j + 1) * TOK, :].reshape(half, WIDE) for core in range(2)
        ]
        both = dot(left_ref[...], jnp.concatenate(parts, axis=0), NT)
        o_ref[j * width : (j + 1) * width, :] = both[:width] + both[width:]
        cut = pl.ds(j * width, width)
        copies.append(pltpu.make_async_copy(o_ref.at[cut], o_hbm.at[cut], sems.at[j]))
        copies[j].start()
    factors = back_ref[:, :, count * TOK :, :].astype(F32)
    factor_ref[...] = jnp.broadcast_to(jnp.sum(factors, axis=(0, 1))[None], factor_ref.shape)
    for copy in copies:
        copy.wait()


def sum_and_copy_kernel(parts_ref, o_ref):
    o_ref[...] = jnp.broadcast_to(jnp.sum(parts_ref[...], axis=0)[None], o_ref.shape)


def unpack_kernel(parts_ref, left_ref, right_ref):
    width, count = left_ref.shape[0], right_ref.shape[0]
    packed = parts_ref[...].reshape(WIDE, WIDE)
    left_ref[...] = packed[:width, :width]
    low = WIDE - width
    right_ref[:low, :] = packed[width:, :count]
    right_ref[low : 2 * low, :] = packed[width:, count:]
    height = count - 2 * low
    lane = lax.broadcasted_iota(jnp.int32, (height, WIDE), 1)
    rest = jnp.zeros((height, WIDE), F32)
    for m in range(-(-count // low)):
        back = pltpu.roll(packed[m * height : (m + 1) * height], WIDE - width + m * low, axis=1)
        rest = jnp.where((lane >= m * low) & (lane < (m + 1) * low), back, rest)
    right_ref[2 * low :, :] = rest[:, :count]


def in_hbm(array):
    return pltpu.with_memory_space_constraint(array, HBM)


def exchange(array, axes):
    return lax.all_to_all(array, axes, split_axis=0, concat_axis=0, tiled=True)


def local(activations, left_factor, right_factor, clip_scale, weight_rows, target):
    tokens, hidden = activations.shape
    width, right_count = left_factor.shape[0], right_factor.shape[0]
    columns = weight_rows.shape[1]
    each = hidden // width
    chips = lax.axis_size(CHIPS)
    owners = 2 * chips
    half = tokens // 2
    rows = right_count * TOK
    other_rows = lax.ppermute(weight_rows, "core", [(0, 1), (1, 0)])

    turned_x, turned_scale = activations.T, clip_scale.T
    by_token, left_parts, back_left, right_parts, scales = call(
        functools.partial(first_kernel, width),
        (
            shape(chips, 2, each, TOK, WIDE),
            shape(WIDE, 2 * WIDE),
            shape(2 * width, WIDE),
            shape(2, 2 * right_count, right_count),
            shape(2, right_count, WIDE, dtype=F32),
        ),
        "first",
        0,
        4 * tokens * hidden,
        in_specs=[pl.BlockSpec(memory_space=HBM)] * 4,
        scratch_shapes=[
            pltpu.VMEM(turned_x.shape, BF16),
            pltpu.VMEM(left_factor.shape, F32),
            pltpu.VMEM(right_factor.shape, F32),
            pltpu.VMEM(turned_scale.shape, F32),
            pltpu.SemaphoreType.DMA((each // 2 + 3,)),
        ],
    )(*map(in_hbm, (turned_x, left_factor, right_factor, turned_scale)))
    moved = exchange(by_token.reshape(owners, each * TOK, WIDE), TENSOR).reshape(rows, WIDE)

    moved, other_rows = lax.optimization_barrier((moved, other_rows))
    lanes_apart = shape(2, rows, LANES, dtype=F32)
    hold = pltpu.VMEM((2, rows, LANES), F32)
    clipped, slope, mixed = call(
        forward_kernel,
        (shape(chips, TOK, 2 * hidden), lanes_apart, lanes_apart),
        "forward",
        10**10,
        12 * rows * width,
        scratch_shapes=[hold],
    )(moved, left_parts, right_parts, scales)
    clipped_back = exchange(clipped, CHIPS)
    partial_out, own_rows = call(
        project_kernel,
        (shape(half, columns), shape(2 * TOK, columns)),
        "project",
        4 * half * hidden * columns,
        4 * hidden * columns,
        vmem=24,
        in_specs=[*[pl.BlockSpec()] * 3, pl.BlockSpec(memory_space=HBM)],
        scratch_shapes=[pltpu.SemaphoreType.DMA(())],
    )(clipped_back, weight_rows, other_rows, in_hbm(target))
    arrived = exchange(partial_out.reshape(chips, TOK, columns), CHIPS)

    grad_copies = call(
        residual_kernel,
        shape(chips, TOK, columns),
        "residual",
        0,
        4 * half * columns,
    )(arrived, own_rows)
    out_grad = exchange(grad_copies, CHIPS).reshape(half, columns)

    turned_grads = [dot(near, out_grad, NT).astype(BF16) for near in (weight_rows, other_rows)]
    clipped_grad = call(
        turn_kernel, shape(half, 2 * hidden), "turn", 0, 8 * half * hidden
    )(*turned_grads)
    grad_owned = exchange(clipped_grad.reshape(chips, TOK, 2 * hidden), CHIPS)

    per_owner = (each + 1) * TOK
    packed = call(
        functools.partial(backward_kernel, width),
        shape(owners, per_owner, WIDE),
        "backward",
        4 * rows * width * width + 12 * rows * width * right_count,
        14 * rows * width,
        scratch_shapes=[hold, hold],
    )(grad_owned, slope, mixed, moved, right_parts)
    back = exchange(packed, TENSOR).reshape(chips, 2, per_owner, WIDE)

    groups = lax.axis_size("dp")
    input_grad, factor_copies = call(
        functools.partial(input_grad_kernel, width),
        (shape(hidden, tokens, dtype=F32), shape(groups, TOK, WIDE, dtype=F32)),
        "input_grad",
        4 * tokens * hidden * width,
        6 * tokens * hidden,
        out_specs=(pl.BlockSpec(memory_space=HBM), pl.BlockSpec()),
        scratch_shapes=[
            pltpu.VMEM((hidden, tokens), F32),
            pltpu.SemaphoreType.DMA((each,)),
        ],
    )(back, back_left)
    factor_parts = exchange(factor_copies, "dp")
    factor_sums = call(
        sum_and_copy_kernel, shape(owners, TOK, WIDE, dtype=F32), "sum_and_copy", 0, 1 << 20
    )(factor_parts)
    gathered = exchange(factor_sums, TENSOR)
    left_sum, right_sum = call(
        unpack_kernel,
        (shape(width, width, dtype=F32), shape(right_count, right_count, dtype=F32)),
        "unpack",
        0,
        1 << 19,
    )(gathered)
    return left_sum, right_sum, input_grad.T


def solution(mesh):
    torus = Mesh(mesh.devices.reshape(mesh.shape["dp"], 4, 4, 2), ("dp", *TENSOR))
    placed = (P("dp", TENSOR), P(), P(), P(), P(TENSOR, None), P("dp", None))
    return jax.shard_map(
        local, mesh=torus, in_specs=placed, out_specs=(P(), P(), P("dp", TENSOR)), check_vma=False
    )
```

```python
import functools

import jax
import jax.numpy as jnp
from jax import lax
from jax.experimental import pallas as pl
from jax.experimental.pallas import tpu as pltpu
from jax.sharding import Mesh
from jax.sharding import PartitionSpec as P

CHIPS = ("chip_x", "chip_y")
TENSOR = (*CHIPS, "core")
F32, BF16 = jnp.float32, jnp.bfloat16
HBM = pltpu.MemorySpace.HBM
TN = (((0,), (0,)), ((), ()))
NT = (((1,), (1,)), ((), ()))
NN = (((1,), (0,)), ((), ()))

LANES, WIDE = 128, 256
TOK = 8


def call(kernel, outs, name, flops=0, moved=0, vmem=16, **kw):
    return pl.pallas_call(
        kernel,
        out_shape=outs,
        compiler_params=pltpu.CompilerParams(vmem_limit_bytes=vmem << 20),
        cost_estimate=pl.CostEstimate(flops=flops, bytes_accessed=moved, transcendentals=0),
        name=name,
        **kw,
    )


def shape(*lengths, dtype=BF16):
    return jax.ShapeDtypeStruct(lengths, dtype)


def halves(a):
    high = a.astype(BF16)
    return high, (a - high.astype(F32)).astype(BF16)


def dot(a, b, dims):
    return lax.dot_general(a, b, dims, preferred_element_type=F32)


def stacked_dot(a, b):
    high, low = b
    count = a.shape[0] // 2
    both = dot(a, high, NN)
    return both[:count] + (both[count:] + dot(a[:count], low, NN))


def of_token(ref, token, count):
    rows = pl.ds(token, count, stride=TOK)
    return jnp.concatenate([ref[0, rows, :], ref[1, rows, :]], axis=1)


def put_token(ref, token, value):
    rows = pl.ds(token, value.shape[0], stride=TOK)
    ref[0, rows, :] = value[:, :LANES]
    ref[1, rows, :] = value[:, LANES:]


def joined(ref):
    return jnp.concatenate([ref[0], ref[1]], axis=1)


def widened(a, rows, value=0.0):
    return jnp.pad(a, ((0, rows - a.shape[0]), (0, WIDE - a.shape[1])), constant_values=value)


def first_kernel(width, *refs):
    *sources, o_ref, left_ref, back_left_ref, right_ref, scale_ref = refs[:9]
    *buffers, sems = refs[9:]
    x_hbm, x_buf = sources[0], buffers[0]
    count = x_hbm.shape[0] // width
    tall = 2 * width
    cuts = [pl.ds(i * tall, tall) for i in range(count // 2)]
    pairs = [(x_hbm.at[cut], x_buf.at[cut]) for cut in cuts] + list(zip(sources[1:], buffers[1:]))
    copies = [
        pltpu.make_async_copy(src, dst, sems.at[i]) for i, (src, dst) in enumerate(pairs)
    ]
    for copy in copies:
        copy.start()
    for j in range(count):
        if j % 2 == 0:
            copies[j // 2].wait()
        part = x_buf[j * width : (j + 1) * width, :].astype(F32)
        part = jnp.pad(part, ((0, WIDE - width), (0, 0)))
        turned = part.T.astype(BF16)
        half = turned.shape[0] // 2
        for core in range(2):
            o_ref[:, core, j] = turned[core * half : (core + 1) * half].reshape(-1, TOK, WIDE)
    for copy in copies[count // 2 :]:
        copy.wait()
    _, left_buf, right_buf, scale_buf = buffers
    high, low = halves(widened(left_buf[...], WIDE))
    left_ref[:, :WIDE] = high
    left_ref[:, WIDE:] = low
    back_left_ref[...] = jnp.concatenate([high[:width], low[:width]], axis=0)
    right_ref[0] = jnp.concatenate(halves(right_buf[...]), axis=0)
    right_ref[1] = jnp.concatenate(halves(right_buf[...].T), axis=0)
    scale = widened(scale_buf[...].T, right_buf.shape[0], 1.0)
    scale_ref[0] = scale
    scale_ref[1] = 1.0 / scale


def forward_kernel(x_ref, left_ref, right_ref, scale_ref, clip_ref, slope_ref, mixed_ref, hold_ref):
    right_count = right_ref.shape[2]
    both = dot(x_ref[...], left_ref[...], NN)
    mixed = both[:, :WIDE] + both[:, WIDE:]
    mixed_ref[0] = mixed[:, :LANES]
    mixed_ref[1] = mixed[:, LANES:]
    turned = right_ref[1]
    scale, inverse = scale_ref[0], scale_ref[1]
    for t in range(TOK):
        rotated = stacked_dot(turned, halves(of_token(mixed_ref, t, right_count)))
        bounded = jnp.tanh(rotated * inverse)
        put_token(hold_ref, t, scale * bounded)
        put_token(slope_ref, t, 1.0 - bounded * bounded)
    core = lax.axis_index("core")
    chips, _, joint = clip_ref.shape
    each = right_count // chips // 2
    width = joint // each // 2
    for chip in range(chips):
        parts = []
        for side in range(2):
            base = chip * 2 * each + lax.rem(core + side, 2) * each
            for j in range(each):
                rows = pl.ds(pl.multiple_of((base + j) * TOK, TOK), TOK)
                parts += [hold_ref[0, rows, :], hold_ref[1, rows, :][:, : width - LANES]]
        clip_ref[chip] = jnp.concatenate(parts, axis=1).astype(BF16)


def own_slot(chips):
    x, y = (lax.axis_index(axis) for axis in CHIPS)
    return lax.axis_index("core") * chips + x * lax.axis_size(CHIPS[1]) + y


def project_kernel(clip_ref, own_ref, other_ref, target_hbm, o_ref, rows_ref, sem):
    chips, _, depth = clip_ref.shape
    hidden, columns = own_ref.shape
    pair = rows_ref.shape[0]
    start = pl.multiple_of(own_slot(chips) // 2 * pair, pair)
    copy = pltpu.make_async_copy(target_hbm.at[pl.ds(start, pair)], rows_ref, sem)
    copy.start()
    part = clip_ref[...].reshape(chips * TOK, depth)
    own, other = part[:, :hidden], part[:, hidden:]
    block = 1024
    for i in range(columns // block):
        cut = slice(i * block, (i + 1) * block)
        total = dot(own, own_ref[:, cut], NN) + dot(other, other_ref[:, cut], NN)
        o_ref[:, cut] = total.astype(BF16)
    copy.wait()


def residual_kernel(parts_ref, rows_ref, o_ref):
    total = jnp.sum(parts_ref[...].astype(F32), axis=0)
    rows = rows_ref[...].astype(F32)
    odd = lax.rem(own_slot(parts_ref.shape[0]), 2) == 1
    own = jnp.where(odd, rows[TOK:], rows[:TOK])
    o_ref[...] = jnp.broadcast_to((total - own).astype(BF16)[None], o_ref.shape)


def turn_kernel(own_ref, other_ref, o_ref):
    hidden = own_ref.shape[0]
    o_ref[:, :hidden] = own_ref[...].T
    o_ref[:, hidden:] = other_ref[...].T


def packed_factors(width, grad_left, grad_right):
    low = WIDE - width
    rest = widened(grad_right[2 * low :], grad_right.shape[0] - 2 * low)
    height = rest.shape[0]
    lane = lax.broadcasted_iota(jnp.int32, (height, WIDE), 1)
    pieces = []
    for m in range(width // height):
        top = grad_left[m * height : (m + 1) * height]
        if m * low < grad_right.shape[1]:
            moved = pltpu.roll(rest, width - m * low, axis=1)
            top = jnp.where(lane < width, top, moved)
        pieces.append(top)
    pieces.append(grad_left[width // height * height : width])
    bottom = jnp.concatenate([grad_right[:low], grad_right[low : 2 * low]], axis=1)
    return jnp.concatenate([*pieces, bottom], axis=0)


def backward_kernel(width, grad_ref, slope_ref, mixed_ref, x_ref, right_ref, o_ref, hold_ref, back_ref):
    right_count = right_ref.shape[2]
    owners = o_ref.shape[0]
    own_rows = x_ref.shape[0] // owners
    core = lax.axis_index("core")
    chips, _, joint = grad_ref.shape
    each = joint // width // 2
    for chip in range(chips):
        rows_of_chip = grad_ref[chip].astype(F32)
        for side in range(2):
            base = chip * 2 * each + lax.rem(core + side, 2) * each
            for j in range(each):
                rows = pl.ds(pl.multiple_of((base + j) * TOK, TOK), TOK)
                start = (side * each + j) * width
                part = widened(rows_of_chip[:, start : start + width], TOK)
                hold_ref[0, rows, :] = part[:, :LANES] * slope_ref[0, rows, :]
                hold_ref[1, rows, :] = part[:, LANES:] * slope_ref[1, rows, :]
    right = right_ref[0]
    grad_right = None
    for t in range(TOK):
        rotated_grad = halves(of_token(hold_ref, t, right_count))
        put_token(back_ref, t, stacked_dot(right, rotated_grad))
        term = dot(of_token(mixed_ref, t, right_count).astype(BF16), rotated_grad[0], NT)
        grad_right = term if grad_right is None else grad_right + term
    mixed_grad = joined(back_ref).astype(BF16)
    grad_left = dot(x_ref[...], mixed_grad, TN)
    o_ref[:, :own_rows, :] = mixed_grad.reshape(owners, own_rows, WIDE)
    packed = packed_factors(width, grad_left, grad_right)
    o_ref[:, own_rows:, :] = packed.reshape(owners, TOK, WIDE).astype(BF16)


def input_grad_kernel(width, back_ref, left_ref, o_hbm, factor_ref, o_ref, sems):
    chips, _, total, _ = back_ref.shape
    count = total // TOK - 1
    half = chips * TOK
    copies = []
    for j in range(count):
        parts = [
            back_ref[:, core, j * TOK : (j + 1) * TOK, :].reshape(half, WIDE) for core in range(2)
        ]
        both = dot(left_ref[...], jnp.concatenate(parts, axis=0), NT)
        o_ref[j * width : (j + 1) * width, :] = both[:width] + both[width:]
        cut = pl.ds(j * width, width)
        copies.append(pltpu.make_async_copy(o_ref.at[cut], o_hbm.at[cut], sems.at[j]))
        copies[j].start()
    factors = back_ref[:, :, count * TOK :, :].astype(F32)
    factor_ref[...] = jnp.broadcast_to(jnp.sum(factors, axis=(0, 1))[None], factor_ref.shape)
    for copy in copies:
        copy.wait()


def sum_and_copy_kernel(parts_ref, o_ref):
    total = jnp.sum(parts_ref[...], axis=0).astype(o_ref.dtype)
    o_ref[...] = jnp.broadcast_to(total[None], o_ref.shape)


def unpack_kernel(parts_ref, left_ref, right_ref):
    width, count = left_ref.shape[0], right_ref.shape[0]
    packed = parts_ref[...].astype(F32).reshape(WIDE, WIDE)
    left_ref[...] = packed[:width, :width]
    low = WIDE - width
    right_ref[:low, :] = packed[width:, :count]
    right_ref[low : 2 * low, :] = packed[width:, count:]
    height = count - 2 * low
    lane = lax.broadcasted_iota(jnp.int32, (height, WIDE), 1)
    rest = jnp.zeros((height, WIDE), F32)
    for m in range(-(-count // low)):
        back = pltpu.roll(packed[m * height : (m + 1) * height], WIDE - width + m * low, axis=1)
        rest = jnp.where((lane >= m * low) & (lane < (m + 1) * low), back, rest)
    right_ref[2 * low :, :] = rest[:, :count]


def in_hbm(array):
    return pltpu.with_memory_space_constraint(array, HBM)


def exchange(array, axes):
    return lax.all_to_all(array, axes, split_axis=0, concat_axis=0, tiled=True)


def local(activations, left_factor, right_factor, clip_scale, weight_rows, target):
    tokens, hidden = activations.shape
    width, right_count = left_factor.shape[0], right_factor.shape[0]
    columns = weight_rows.shape[1]
    each = hidden // width
    chips = lax.axis_size(CHIPS)
    owners = 2 * chips
    half = tokens // 2
    rows = right_count * TOK
    other_rows = lax.ppermute(weight_rows, "core", [(0, 1), (1, 0)])

    turned_x, turned_scale = activations.T, clip_scale.T
    by_token, left_parts, back_left, right_parts, scales = call(
        functools.partial(first_kernel, width),
        (
            shape(chips, 2, each, TOK, WIDE),
            shape(WIDE, 2 * WIDE),
            shape(2 * width, WIDE),
            shape(2, 2 * right_count, right_count),
            shape(2, right_count, WIDE, dtype=F32),
        ),
        "first",
        0,
        4 * tokens * hidden,
        in_specs=[pl.BlockSpec(memory_space=HBM)] * 4,
        scratch_shapes=[
            pltpu.VMEM(turned_x.shape, BF16),
            pltpu.VMEM(left_factor.shape, F32),
            pltpu.VMEM(right_factor.shape, F32),
            pltpu.VMEM(turned_scale.shape, F32),
            pltpu.SemaphoreType.DMA((each // 2 + 3,)),
        ],
    )(*map(in_hbm, (turned_x, left_factor, right_factor, turned_scale)))
    moved = exchange(by_token.reshape(owners, each * TOK, WIDE), TENSOR).reshape(rows, WIDE)

    moved, other_rows = lax.optimization_barrier((moved, other_rows))
    lanes_apart = shape(2, rows, LANES, dtype=F32)
    hold = pltpu.VMEM((2, rows, LANES), F32)
    clipped, slope, mixed = call(
        forward_kernel,
        (shape(chips, TOK, 2 * hidden), lanes_apart, lanes_apart),
        "forward",
        10**10,
        12 * rows * width,
        scratch_shapes=[hold],
    )(moved, left_parts, right_parts, scales)
    clipped_back = exchange(clipped, CHIPS)
    partial_out, own_rows = call(
        project_kernel,
        (shape(half, columns), shape(2 * TOK, columns)),
        "project",
        4 * half * hidden * columns,
        4 * hidden * columns,
        vmem=24,
        in_specs=[*[pl.BlockSpec()] * 3, pl.BlockSpec(memory_space=HBM)],
        scratch_shapes=[pltpu.SemaphoreType.DMA(())],
    )(clipped_back, weight_rows, other_rows, in_hbm(target))
    arrived = exchange(partial_out.reshape(chips, TOK, columns), CHIPS)

    grad_copies = call(
        residual_kernel,
        shape(chips, TOK, columns),
        "residual",
        0,
        4 * half * columns,
    )(arrived, own_rows)
    out_grad = exchange(grad_copies, CHIPS).reshape(half, columns)

    turned_grads = [dot(near, out_grad, NT).astype(BF16) for near in (weight_rows, other_rows)]
    clipped_grad = call(
        turn_kernel, shape(half, 2 * hidden), "turn", 0, 8 * half * hidden
    )(*turned_grads)
    grad_owned = exchange(clipped_grad.reshape(chips, TOK, 2 * hidden), CHIPS)

    per_owner = (each + 1) * TOK
    packed = call(
        functools.partial(backward_kernel, width),
        shape(owners, per_owner, WIDE),
        "backward",
        4 * rows * width * width + 12 * rows * width * right_count,
        14 * rows * width,
        scratch_shapes=[hold, hold],
    )(grad_owned, slope, mixed, moved, right_parts)
    back = exchange(packed, TENSOR).reshape(chips, 2, per_owner, WIDE)

    groups = lax.axis_size("dp")
    input_grad, factor_copies = call(
        functools.partial(input_grad_kernel, width),
        (shape(hidden, tokens, dtype=F32), shape(groups, TOK, WIDE, dtype=F32)),
        "input_grad",
        4 * tokens * hidden * width,
        6 * tokens * hidden,
        out_specs=(pl.BlockSpec(memory_space=HBM), pl.BlockSpec()),
        scratch_shapes=[
            pltpu.VMEM((hidden, tokens), F32),
            pltpu.SemaphoreType.DMA((each,)),
        ],
    )(back, back_left)
    factor_parts = exchange(factor_copies, "dp")
    factor_sums = call(
        sum_and_copy_kernel, shape(owners, TOK, WIDE), "sum_and_copy", 0, 1 << 20
    )(factor_parts)
    gathered = exchange(factor_sums, TENSOR)
    left_sum, right_sum = call(
        unpack_kernel,
        (shape(width, width, dtype=F32), shape(right_count, right_count, dtype=F32)),
        "unpack",
        0,
        1 << 19,
    )(gathered)
    return left_sum, right_sum, input_grad.T


def solution(mesh):
    torus = Mesh(mesh.devices.reshape(mesh.shape["dp"], 4, 4, 2), ("dp", *TENSOR))
    placed = (P("dp", TENSOR), P(), P(), P(), P(TENSOR, None), P("dp", None))
    return jax.shard_map(
        local, mesh=torus, in_specs=placed, out_specs=(P(), P(), P("dp", TENSOR)), check_vma=False
    )
```

```python
import functools

import jax
import jax.numpy as jnp
from jax import lax
from jax.experimental import pallas as pl
from jax.experimental.pallas import tpu as pltpu
from jax.sharding import Mesh
from jax.sharding import PartitionSpec as P

CHIPS = ("chip_x", "chip_y")
TENSOR = (*CHIPS, "core")
F32, BF16 = jnp.float32, jnp.bfloat16
HBM = pltpu.MemorySpace.HBM
TN = (((0,), (0,)), ((), ()))
NT = (((1,), (1,)), ((), ()))
NN = (((1,), (0,)), ((), ()))

LANES, WIDE = 128, 256
TOK = 8


def call(kernel, outs, name, flops=0, moved=0, vmem=16, **kw):
    return pl.pallas_call(
        kernel,
        out_shape=outs,
        compiler_params=pltpu.CompilerParams(vmem_limit_bytes=vmem << 20),
        cost_estimate=pl.CostEstimate(flops=flops, bytes_accessed=moved, transcendentals=0),
        name=name,
        **kw,
    )


def shape(*lengths, dtype=BF16):
    return jax.ShapeDtypeStruct(lengths, dtype)


def halves(a):
    high = a.astype(BF16)
    return high, (a - high.astype(F32)).astype(BF16)


def dot(a, b, dims):
    return lax.dot_general(a, b, dims, preferred_element_type=F32)


def stacked_dot(a, b):
    high, low = b
    count = a.shape[0] // 2
    both = dot(a, high, NN)
    return both[:count] + (both[count:] + dot(a[:count], low, NN))


def of_token(ref, token, count):
    rows = pl.ds(token, count, stride=TOK)
    return jnp.concatenate([ref[0, rows, :], ref[1, rows, :]], axis=1)


def put_token(ref, token, value):
    rows = pl.ds(token, value.shape[0], stride=TOK)
    ref[0, rows, :] = value[:, :LANES]
    ref[1, rows, :] = value[:, LANES:]


def joined(ref):
    return jnp.concatenate([ref[0], ref[1]], axis=1)


def widened(a, rows, value=0.0):
    return jnp.pad(a, ((0, rows - a.shape[0]), (0, WIDE - a.shape[1])), constant_values=value)


def first_kernel(width, *refs):
    *sources, o_ref, left_ref, back_left_ref, right_ref, scale_ref = refs[:9]
    *buffers, sems = refs[9:]
    x_hbm, x_buf = sources[0], buffers[0]
    count = x_hbm.shape[0] // width
    tall = 2 * width
    cuts = [pl.ds(i * tall, tall) for i in range(count // 2)]
    pairs = [(x_hbm.at[cut], x_buf.at[cut]) for cut in cuts] + list(zip(sources[1:], buffers[1:]))
    copies = [
        pltpu.make_async_copy(src, dst, sems.at[i]) for i, (src, dst) in enumerate(pairs)
    ]
    for copy in copies:
        copy.start()
    for j in range(count):
        if j % 2 == 0:
            copies[j // 2].wait()
        part = x_buf[j * width : (j + 1) * width, :].astype(F32)
        part = jnp.pad(part, ((0, WIDE - width), (0, 0)))
        turned = part.T.astype(BF16)
        half = turned.shape[0] // 2
        for core in range(2):
            o_ref[:, core, j] = turned[core * half : (core + 1) * half].reshape(-1, TOK, WIDE)
    for copy in copies[count // 2 :]:
        copy.wait()
    _, left_buf, right_buf, scale_buf = buffers
    high, low = halves(widened(left_buf[...], WIDE))
    left_ref[:, :WIDE] = high
    left_ref[:, WIDE:] = low
    back_left_ref[...] = jnp.concatenate([high[:width], low[:width]], axis=0)
    right_ref[0] = jnp.concatenate(halves(right_buf[...]), axis=0)
    right_ref[1] = jnp.concatenate(halves(right_buf[...].T), axis=0)
    scale = widened(scale_buf[...].T, right_buf.shape[0], 1.0)
    scale_ref[0] = scale
    scale_ref[1] = 1.0 / scale


def forward_kernel(x_ref, left_ref, right_ref, scale_ref, clip_ref, slope_ref, mixed_ref, hold_ref):
    right_count = right_ref.shape[2]
    both = dot(x_ref[...], left_ref[...], NN)
    mixed = both[:, :WIDE] + both[:, WIDE:]
    mixed_ref[0] = mixed[:, :LANES]
    mixed_ref[1] = mixed[:, LANES:]
    turned = right_ref[1]
    scale, inverse = scale_ref[0], scale_ref[1]
    for t in range(TOK):
        rotated = stacked_dot(turned, halves(of_token(mixed_ref, t, right_count)))
        bounded = jnp.tanh(rotated * inverse)
        put_token(hold_ref, t, scale * bounded)
        put_token(slope_ref, t, 1.0 - bounded * bounded)
    core = lax.axis_index("core")
    chips, _, joint = clip_ref.shape
    each = right_count // chips // 2
    width = joint // each // 2
    for chip in range(chips):
        parts = []
        for side in range(2):
            base = chip * 2 * each + lax.rem(core + side, 2) * each
            for j in range(each):
                rows = pl.ds(pl.multiple_of((base + j) * TOK, TOK), TOK)
                parts += [hold_ref[0, rows, :], hold_ref[1, rows, :][:, : width - LANES]]
        clip_ref[chip] = jnp.concatenate(parts, axis=1).astype(BF16)


def own_slot(chips):
    x, y = (lax.axis_index(axis) for axis in CHIPS)
    return lax.axis_index("core") * chips + x * lax.axis_size(CHIPS[1]) + y


def project_kernel(clip_ref, own_ref, other_ref, target_hbm, o_ref, rows_ref, sem):
    chips, _, depth = clip_ref.shape
    hidden, columns = own_ref.shape
    pair = rows_ref.shape[0]
    start = pl.multiple_of(own_slot(chips) // 2 * pair, pair)
    copy = pltpu.make_async_copy(target_hbm.at[pl.ds(start, pair)], rows_ref, sem)
    copy.start()
    part = clip_ref[...].reshape(chips * TOK, depth)
    own, other = part[:, :hidden], part[:, hidden:]
    block = 1024
    for i in range(columns // block):
        cut = slice(i * block, (i + 1) * block)
        total = dot(own, own_ref[:, cut], NN) + dot(other, other_ref[:, cut], NN)
        o_ref[:, cut] = total.astype(BF16)
    copy.wait()


def residual_kernel(parts_ref, rows_ref, o_ref):
    total = jnp.sum(parts_ref[...].astype(F32), axis=0)
    rows = rows_ref[...].astype(F32)
    odd = lax.rem(own_slot(parts_ref.shape[0]), 2) == 1
    own = jnp.where(odd, rows[TOK:], rows[:TOK])
    o_ref[...] = jnp.broadcast_to((total - own).astype(BF16)[None], o_ref.shape)


def turn_kernel(own_ref, other_ref, o_ref):
    hidden = own_ref.shape[0]
    o_ref[:, :hidden] = own_ref[...].T
    o_ref[:, hidden:] = other_ref[...].T


def packed_factors(width, grad_left, grad_right):
    low = WIDE - width
    rest = widened(grad_right[2 * low :], grad_right.shape[0] - 2 * low)
    height = rest.shape[0]
    lane = lax.broadcasted_iota(jnp.int32, (height, WIDE), 1)
    pieces = []
    for m in range(width // height):
        top = grad_left[m * height : (m + 1) * height]
        if m * low < grad_right.shape[1]:
            moved = pltpu.roll(rest, width - m * low, axis=1)
            top = jnp.where(lane < width, top, moved)
        pieces.append(top)
    pieces.append(grad_left[width // height * height : width])
    bottom = jnp.concatenate([grad_right[:low], grad_right[low : 2 * low]], axis=1)
    return jnp.concatenate([*pieces, bottom], axis=0)


def backward_kernel(width, grad_ref, slope_ref, mixed_ref, x_ref, right_ref, o_ref, hold_ref, back_ref):
    right_count = right_ref.shape[2]
    owners = o_ref.shape[0]
    own_rows = x_ref.shape[0] // owners
    core = lax.axis_index("core")
    chips, _, joint = grad_ref.shape
    each = joint // width // 2
    for chip in range(chips):
        rows_of_chip = grad_ref[chip].astype(F32)
        for side in range(2):
            base = chip * 2 * each + lax.rem(core + side, 2) * each
            for j in range(each):
                rows = pl.ds(pl.multiple_of((base + j) * TOK, TOK), TOK)
                start = (side * each + j) * width
                part = widened(rows_of_chip[:, start : start + width], TOK)
                hold_ref[0, rows, :] = part[:, :LANES] * slope_ref[0, rows, :]
                hold_ref[1, rows, :] = part[:, LANES:] * slope_ref[1, rows, :]
    right = right_ref[0]
    grad_right = None
    for t in range(TOK):
        rotated_grad = halves(of_token(hold_ref, t, right_count))
        put_token(back_ref, t, stacked_dot(right, rotated_grad))
        term = dot(of_token(mixed_ref, t, right_count).astype(BF16), rotated_grad[0], NT)
        grad_right = term if grad_right is None else grad_right + term
    mixed_grad = joined(back_ref).astype(BF16)
    grad_left = dot(x_ref[...], mixed_grad, TN)
    o_ref[:, :own_rows, :] = mixed_grad.reshape(owners, own_rows, WIDE)
    packed = packed_factors(width, grad_left, grad_right)
    o_ref[:, own_rows:, :] = packed.reshape(owners, TOK, WIDE).astype(BF16)


def plane_sum_kernel(back_ref, factor_ref):
    factors = back_ref[:, -TOK:, :].astype(F32)
    factor_ref[...] = jnp.broadcast_to(jnp.sum(factors, axis=0)[None], factor_ref.shape)


def input_grad_kernel(width, back_ref, left_ref, o_hbm, o_ref, sems):
    chips, _, total, _ = back_ref.shape
    count = total // TOK - 1
    half = chips * TOK
    copies = []
    for j in range(count):
        parts = [
            back_ref[:, core, j * TOK : (j + 1) * TOK, :].reshape(half, WIDE) for core in range(2)
        ]
        both = dot(left_ref[...], jnp.concatenate(parts, axis=0), NT)
        o_ref[j * width : (j + 1) * width, :] = both[:width] + both[width:]
        cut = pl.ds(j * width, width)
        copies.append(pltpu.make_async_copy(o_ref.at[cut], o_hbm.at[cut], sems.at[j]))
        copies[j].start()
    for copy in copies:
        copy.wait()


def sum_and_copy_kernel(parts_ref, o_ref):
    total = jnp.sum(parts_ref[...], axis=0).astype(o_ref.dtype)
    o_ref[...] = jnp.broadcast_to(total[None], o_ref.shape)


def unpack_kernel(parts_ref, left_ref, right_ref):
    width, count = left_ref.shape[0], right_ref.shape[0]
    packed = parts_ref[...].astype(F32).reshape(WIDE, WIDE)
    left_ref[...] = packed[:width, :width]
    low = WIDE - width
    right_ref[:low, :] = packed[width:, :count]
    right_ref[low : 2 * low, :] = packed[width:, count:]
    height = count - 2 * low
    lane = lax.broadcasted_iota(jnp.int32, (height, WIDE), 1)
    rest = jnp.zeros((height, WIDE), F32)
    for m in range(-(-count // low)):
        back = pltpu.roll(packed[m * height : (m + 1) * height], WIDE - width + m * low, axis=1)
        rest = jnp.where((lane >= m * low) & (lane < (m + 1) * low), back, rest)
    right_ref[2 * low :, :] = rest[:, :count]


def in_hbm(array):
    return pltpu.with_memory_space_constraint(array, HBM)


def exchange(array, axes):
    return lax.all_to_all(array, axes, split_axis=0, concat_axis=0, tiled=True)


def local(activations, left_factor, right_factor, clip_scale, weight_rows, target):
    tokens, hidden = activations.shape
    width, right_count = left_factor.shape[0], right_factor.shape[0]
    columns = weight_rows.shape[1]
    each = hidden // width
    chips = lax.axis_size(CHIPS)
    owners = 2 * chips
    half = tokens // 2
    rows = right_count * TOK
    other_rows = lax.ppermute(weight_rows, "core", [(0, 1), (1, 0)])

    turned_x, turned_scale = activations.T, clip_scale.T
    by_token, left_parts, back_left, right_parts, scales = call(
        functools.partial(first_kernel, width),
        (
            shape(chips, 2, each, TOK, WIDE),
            shape(WIDE, 2 * WIDE),
            shape(2 * width, WIDE),
            shape(2, 2 * right_count, right_count),
            shape(2, right_count, WIDE, dtype=F32),
        ),
        "first",
        0,
        4 * tokens * hidden,
        in_specs=[pl.BlockSpec(memory_space=HBM)] * 4,
        scratch_shapes=[
            pltpu.VMEM(turned_x.shape, BF16),
            pltpu.VMEM(left_factor.shape, F32),
            pltpu.VMEM(right_factor.shape, F32),
            pltpu.VMEM(turned_scale.shape, F32),
            pltpu.SemaphoreType.DMA((each // 2 + 3,)),
        ],
    )(*map(in_hbm, (turned_x, left_factor, right_factor, turned_scale)))
    moved = exchange(by_token.reshape(owners, each * TOK, WIDE), TENSOR).reshape(rows, WIDE)

    moved, other_rows = lax.optimization_barrier((moved, other_rows))
    lanes_apart = shape(2, rows, LANES, dtype=F32)
    hold = pltpu.VMEM((2, rows, LANES), F32)
    clipped, slope, mixed = call(
        forward_kernel,
        (shape(chips, TOK, 2 * hidden), lanes_apart, lanes_apart),
        "forward",
        10**10,
        12 * rows * width,
        scratch_shapes=[hold],
    )(moved, left_parts, right_parts, scales)
    clipped_back = exchange(clipped, CHIPS)
    partial_out, own_rows = call(
        project_kernel,
        (shape(half, columns), shape(2 * TOK, columns)),
        "project",
        4 * half * hidden * columns,
        4 * hidden * columns,
        vmem=24,
        in_specs=[*[pl.BlockSpec()] * 3, pl.BlockSpec(memory_space=HBM)],
        scratch_shapes=[pltpu.SemaphoreType.DMA(())],
    )(clipped_back, weight_rows, other_rows, in_hbm(target))
    arrived = exchange(partial_out.reshape(chips, TOK, columns), CHIPS)

    grad_copies = call(
        residual_kernel,
        shape(chips, TOK, columns),
        "residual",
        0,
        4 * half * columns,
    )(arrived, own_rows)
    out_grad = exchange(grad_copies, CHIPS).reshape(half, columns)

    turned_grads = [dot(near, out_grad, NT).astype(BF16) for near in (weight_rows, other_rows)]
    clipped_grad = call(
        turn_kernel, shape(half, 2 * hidden), "turn", 0, 8 * half * hidden
    )(*turned_grads)
    grad_owned = exchange(clipped_grad.reshape(chips, TOK, 2 * hidden), CHIPS)

    per_owner = (each + 1) * TOK
    packed = call(
        functools.partial(backward_kernel, width),
        shape(owners, per_owner, WIDE),
        "backward",
        4 * rows * width * width + 12 * rows * width * right_count,
        14 * rows * width,
        scratch_shapes=[hold, hold],
    )(grad_owned, slope, mixed, moved, right_parts)
    back = exchange(packed, TENSOR)

    groups = lax.axis_size("dp")
    factor_copies = call(
        plane_sum_kernel, shape(groups, TOK, WIDE, dtype=F32), "plane_sum", 0, 1 << 18
    )(back)
    factor_parts = exchange(factor_copies, "dp")
    input_grad = call(
        functools.partial(input_grad_kernel, width),
        shape(hidden, tokens, dtype=F32),
        "input_grad",
        4 * tokens * hidden * width,
        6 * tokens * hidden,
        out_specs=pl.BlockSpec(memory_space=HBM),
        scratch_shapes=[
            pltpu.VMEM((hidden, tokens), F32),
            pltpu.SemaphoreType.DMA((each,)),
        ],
    )(back.reshape(chips, 2, per_owner, WIDE), back_left)
    factor_sums = call(
        sum_and_copy_kernel, shape(owners, TOK, WIDE), "sum_and_copy", 0, 1 << 20
    )(factor_parts)
    gathered = exchange(factor_sums, TENSOR)
    left_sum, right_sum = call(
        unpack_kernel,
        (shape(width, width, dtype=F32), shape(right_count, right_count, dtype=F32)),
        "unpack",
        0,
        1 << 19,
    )(gathered)
    return left_sum, right_sum, input_grad.T


def solution(mesh):
    torus = Mesh(mesh.devices.reshape(mesh.shape["dp"], 4, 4, 2), ("dp", *TENSOR))
    placed = (P("dp", TENSOR), P(), P(), P(), P(TENSOR, None), P("dp", None))
    return jax.shard_map(
        local, mesh=torus, in_specs=placed, out_specs=(P(), P(), P("dp", TENSOR)), check_vma=False
    )
```
